32 devices in a mesh: row: 2 (over y), col: 16 (over z, x, core).
Axes of the slice: x: 2, y: 2, z: 4, core: 2. Of those that a mesh axis runs over, the one named last changes fastest.
Arguments:
- x_field: bfloat16 [65536, 256], P('col'), may hold values from -6 to 6
- observed: bfloat16 [2048, 256], P(('row', 'col')), may hold values from -6 to 6
- sat_scale: float32 [256], replicated, may hold values from 0.5 to 4
- u_coef: bfloat16 [4, 128, 512, 256], P('row', 'col'), may hold values from -0.046875 to 0.046875
- v_coef: bfloat16 [4, 128, 512, 256], P('row', 'col'), may hold values from -0.25 to 0.25
- ranks: int32 [4, 128], P('row', 'col'), may hold values from 16 to 256
Outputs:
- gradient: bfloat16 [65536, 256], P('col')
The draws below stay inside these ranges and needn't reach their ends.
All inputs are finite; a program needn't handle non-finite values.
Results may differ from the reference program's by a relative error of at most 0.0065.
Values may be sent and summed in bfloat16 or wider, within the bound.
No kernel may reach another device: no remote copies, remote signals or barrier semaphores. Data moves between devices by JAX's collectives and lax.ppermute only.
A program may use at most 64 MiB of HBM per device.

```python
import math
import jax
import jax.numpy as jnp
from jax import lax

TILE = 512
RMAX = 256
S = 256
NT_ROWS = 4
NT_COLS = 128
ROWS = 2048
NCOLS = 65536


def plant(values, own_key, low, largest):
    spot = [jax.random.randint(jax.random.fold_in(own_key, axis), (), 0, length) for axis, length in enumerate(values.shape)]
    widest = values.shape.index(max(values.shape))
    beside = spot[:widest] + [(spot[widest] + 1) % values.shape[widest]] + spot[widest + 1:]
    return values.at[tuple(spot)].set(low).at[tuple(beside)].set(largest)


def block_scale(rng, extent, pieces, least, top_value):
    loudness, own = 1.0, jax.random.fold_in(rng, 6)
    for dim, parts in pieces:
        draws = jnp.exp(jax.random.uniform(jax.random.fold_in(own, dim), (parts,), jnp.float32, least / len(pieces), top_value / len(pieces)))
        loudness = loudness * jnp.repeat(draws, extent[dim] // parts).reshape([-1 if axis == dim else 1 for axis in range(len(extent))])
    return loudness


def centred(rng, dims, deviation, limit, pieces=(), held_as=jnp.bfloat16):
    array = jax.random.normal(rng, dims, jnp.float32) * deviation
    if len(pieces) > 0:
        array = block_scale(rng, dims, pieces, -0.22, 0.18) * array
    return jnp.clip(array, min=-limit, max=limit).astype(held_as)


def setup_inputs(seed: int = 0) -> dict:
    key_list = jax.random.split(jax.random.key(seed), 7)
    x_field = centred(key_list[0], (NCOLS, S), 1.0, 6.0, ((0, 16),))
    observed = centred(key_list[1], (ROWS, S), 1.0, 6.0, ((0, 32),))
    sat_scale = jnp.clip(jnp.exp(jax.random.uniform(key_list[2], (S,), jnp.float32, math.log(0.5), math.log(4.0))), 0.5, 4.0)
    u_coef = centred(key_list[3], (NT_ROWS, NT_COLS, TILE, RMAX), (NT_COLS * RMAX // 2) ** -0.5, 0.046875, ((0, 2), (1, 16)))
    v_coef = centred(key_list[4], (NT_ROWS, NT_COLS, TILE, RMAX), TILE ** -0.5, 0.25, ((0, 2), (1, 16)))
    ranks = plant(jax.random.randint(key_list[5], (NT_ROWS, NT_COLS), RMAX // 16, RMAX + 1), jax.random.fold_in(key_list[5], 1), RMAX // 16, RMAX).astype(jnp.int32)
    return {"x_field": x_field, "observed": observed, "sat_scale": sat_scale, "u_coef": u_coef, "v_coef": v_coef, "ranks": ranks}


def reference(x_field, observed, sat_scale, u_coef, v_coef, ranks):
    source_tiles = x_field.astype(jnp.float32).reshape(NT_COLS, TILE, S)
    rank_mask = (jnp.arange(RMAX, dtype=jnp.int32)[None, None, :] < ranks[:, :, None]).astype(jnp.float32)[..., None]

    def forward_row(packed):
        u_tile, v_tile, mask_row = packed
        coeffs = jnp.einsum("jtk,jts->jks", v_tile.astype(jnp.float32), source_tiles)
        coeffs = (coeffs * mask_row).astype(jnp.bfloat16)
        return jnp.einsum("jtk,jks->ts", u_tile.astype(jnp.float32), coeffs.astype(jnp.float32))

    predicted = lax.map(forward_row, (u_coef, v_coef, rank_mask)).reshape(ROWS, S)
    misfit = (predicted - observed.astype(jnp.float32)) / sat_scale
    residual = (sat_scale * jnp.tanh(misfit)).astype(jnp.bfloat16)
    resid_tiles = residual.reshape(NT_ROWS, TILE, S)

    def adjoint_row(running, packed):
        u_tile, v_tile, mask_row, resid_row = packed
        adjoint = jnp.einsum("jtk,ts->jks", u_tile.astype(jnp.float32), resid_row.astype(jnp.float32))
        adjoint = (adjoint * mask_row).astype(jnp.bfloat16)
        return running + jnp.einsum("jtk,jks->jts", v_tile.astype(jnp.float32), adjoint.astype(jnp.float32)), None

    gradient, _ = lax.scan(adjoint_row, jnp.zeros((NT_COLS, TILE, S), jnp.float32), (u_coef, v_coef, rank_mask, resid_tiles))
    return gradient.reshape(NCOLS, S).astype(jnp.bfloat16)
```

```python
import functools

import jax
import jax.numpy as jnp
from jax import lax
from jax.experimental import pallas as pl
from jax.experimental.pallas import tpu as pltpu
from jax.sharding import PartitionSpec as P

BF = jnp.bfloat16
F32 = jnp.float32
CUTS = (64, 64, 128)
GROUPS = 4


def dot_nn(a, b):
    return lax.dot_general(a, b, (((1,), (0,)), ((), ())), preferred_element_type=F32)


def dot_nt(a, b):
    return lax.dot_general(a, b, (((1,), (1,)), ((), ())), preferred_element_type=F32)


def permuted_rows(tile, quads, zs, rb):
    return jnp.concatenate(
        [tile[(z * quads + q) * rb : (z * quads + q + 1) * rb] for q in range(quads) for z in range(zs)], axis=0
    )


def forward_kernel(dims, ranks, me, x_ref, u_ref, v_ref, *rest):
    tile_rows, jb, width, cap, sources, rb, zs, cuts = dims
    n = len(cuts)
    keep_refs, send_refs, acc = rest[:n], rest[n : 2 * n], rest[2 * n]
    step = pl.program_id(0)
    cols = pl.num_programs(0) * jb
    lane = lax.broadcasted_iota(jnp.int32, (sources, cap), 1)
    parts = [[] for _ in range(tile_rows)]
    for jj in range(jb):
        xt = x_ref[jj * width : (jj + 1) * width, :].T
        for a in range(tile_rows):
            c = dot_nn(xt, v_ref[a, jj])
            c = jnp.where(lane < ranks[a * cols + step * jb + jj], c, 0.0).astype(BF)
            parts[a].append(c)
    for a in range(tile_rows):
        c = jnp.concatenate(parts[a], axis=1)
        w = jnp.concatenate([permuted_rows(u_ref[a, jj], 4, zs, rb) for jj in range(jb)], axis=1)
        p = dot_nt(c, w)

        @pl.when(step == 0)
        def _():
            acc[a] = p

        @pl.when(step > 0)
        def _():
            acc[a] += p

    @pl.when(step == pl.num_programs(0) - 1)
    def _():
        mine, my_x = me[0], me[1]
        q_lanes = width // 4
        for q in range(4):
            qx, qc = q // 2, q % 2
            slot = qx ^ my_x
            row = 0
            for i, s in enumerate(cuts):
                for a in range(tile_rows):
                    val = acc[a, row : row + s, q * q_lanes : (q + 1) * q_lanes]

                    @pl.when(mine == qc)
                    def _():
                        keep_refs[i][slot, :, a * q_lanes : (a + 1) * q_lanes] = val

                    @pl.when(mine != qc)
                    def _():
                        send_refs[i][slot, :, a * q_lanes : (a + 1) * q_lanes] = val.astype(BF)

                row += s


def forward(x, u, v, ranks, me, cuts, rb, zs):
    tile_rows, tile_cols, width, cap = u.shape
    sources = x.shape[1]
    jb = 2 if tile_cols % 2 == 0 else 1
    block = tile_rows * width // 4
    dims = (tile_rows, jb, width, cap, sources, rb, zs, cuts)
    outs = [jax.ShapeDtypeStruct((2, s, block), F32) for s in cuts] + [
        jax.ShapeDtypeStruct((2, s, block), BF) for s in cuts
    ]
    whole = [pl.BlockSpec((2, s, block), lambda j, *_: (0, 0, 0)) for s in cuts]
    res = pl.pallas_call(
        functools.partial(forward_kernel, dims),
        grid_spec=pltpu.PrefetchScalarGridSpec(
            num_scalar_prefetch=2,
            grid=(tile_cols // jb,),
            in_specs=[
                pl.BlockSpec((jb * width, sources), lambda j, *_: (j, 0)),
                pl.BlockSpec((tile_rows, jb, width, cap), lambda j, *_: (0, j, 0, 0)),
                pl.BlockSpec((tile_rows, jb, width, cap), lambda j, *_: (0, j, 0, 0)),
            ],
            out_specs=whole + whole,
            scratch_shapes=[pltpu.VMEM((tile_rows, sources, width), F32)],
        ),
        out_shape=outs,
        cost_estimate=pl.CostEstimate(
            flops=4 * tile_rows * tile_cols * width * cap * sources,
            bytes_accessed=4 * u.size + 2 * x.size,
            transcendentals=0,
        ),
        name="forward",
    )(ranks.reshape(-1), me, x, u, v)
    return res[: len(cuts)], res[len(cuts) :]


def adjoint_kernel(dims, ranks, me, r00, r01, r10, r11, u_ref, v_ref, g_ref, held):
    tile_rows, tile_cols, start, width, cap, s, rb, zs = dims
    j = pl.program_id(0)

    @pl.when(j == 0)
    def _():
        base = me[1] * 2 + me[0]
        held[base] = r00[...]
        held[base ^ 2] = r01[...]
        held[base ^ 1] = r10[...]
        held[base ^ 3] = r11[...]

    q_lanes = width // 4
    lane = lax.broadcasted_iota(jnp.int32, (s, cap), 1)
    total = None
    for a in range(tile_rows):
        r = jnp.concatenate([held[q][:, a * q_lanes : (a + 1) * q_lanes] for q in range(4)], axis=1)
        adj = dot_nn(r, permuted_rows(u_ref[a, 0], 4, zs, rb))
        adj = jnp.where(lane < ranks[a * tile_cols + start + j], adj, 0.0).astype(BF)
        g = dot_nt(adj, v_ref[a, 0])
        total = g if total is None else total + g
    g_ref[0] = total.astype(BF)


def adjoint(rs, u, v, ranks, me, start, count, rb, zs):
    tile_rows, tile_cols, width, cap = u.shape
    s, block = rs[0].shape
    dims = (tile_rows, tile_cols, start, width, cap, s, rb, zs)
    small = pl.BlockSpec((s, block), lambda j, *_: (0, 0))
    tiles = pl.BlockSpec((tile_rows, 1, width, cap), lambda j, *_: (0, start + j, 0, 0))
    return pl.pallas_call(
        functools.partial(adjoint_kernel, dims),
        grid_spec=pltpu.PrefetchScalarGridSpec(
            num_scalar_prefetch=2,
            grid=(count,),
            in_specs=[small] * 4 + [tiles, tiles],
            out_specs=pl.BlockSpec((1, s, width), lambda j, *_: (j, 0, 0)),
            scratch_shapes=[pltpu.VMEM((4, s, block), BF)],
        ),
        out_shape=jax.ShapeDtypeStruct((count, s, width), BF),
        cost_estimate=pl.CostEstimate(
            flops=4 * tile_rows * count * width * cap * s,
            bytes_accessed=4 * u.size * count // tile_cols,
            transcendentals=0,
        ),
        name="adjoint",
    )(ranks.reshape(-1), me, *rs, u, v)


def finish_kernel(n, *refs):
    out = refs[-1]
    for i in range(n):
        a, b = refs[2 * i], refs[2 * i + 1]
        s = a.shape[1]
        t = (a[0].astype(F32) + b[0].astype(F32)).astype(BF)
        out[:, i * s : (i + 1) * s] = t.T


def finish(out, pairs, start, lane_block, rows, sources):
    count, s, width = pairs[0][0].shape
    n = len(pairs)
    piece = pl.BlockSpec((1, s, width), lambda j: (j, 0, 0))
    flat = [p for pair in pairs for p in pair]
    lanes = n * s
    aliases = {}
    specs = [piece] * len(flat)
    body = functools.partial(finish_kernel, n)
    if out is not None:
        aliases = {len(flat): 0}
        specs = specs + [pl.BlockSpec(memory_space=pl.ANY)]
        inner = body
        body = lambda *refs: inner(*refs[: len(flat)], refs[-1])
        flat = flat + [out]
    return pl.pallas_call(
        body,
        grid=(count,),
        in_specs=specs,
        out_specs=pl.BlockSpec((width, lanes), lambda j: (start + j, lane_block)),
        out_shape=jax.ShapeDtypeStruct((rows, sources), BF),
        input_output_aliases=aliases,
        cost_estimate=pl.CostEstimate(flops=0, bytes_accessed=6 * count * lanes * width, transcendentals=0),
        name="finish",
    )(*flat)


def solution(mesh):
    n_row, n_col = mesh.shape["row"], mesh.shape["col"]
    nz = n_col // 4
    assert n_col == 4 * nz and nz & (nz - 1) == 0
    core_swap = [(c, c ^ 1) for c in range(n_col)]
    x_swap = [(c, c ^ 2) for c in range(n_col)]
    z_swaps = [[(c, c ^ (4 * k)) for c in range(n_col)] for k in range(1, nz)]
    row_swap = [(0, 1), (1, 0)]

    def local(x_field, observed, sat_scale, u, v, ranks):
        tile_rows, tile_cols, width, cap = u.shape
        rows, sources = x_field.shape
        rb = observed.shape[0]
        zs = nz // tile_rows
        cuts = tuple(c * sources // 256 for c in CUTS)
        me_col = lax.axis_index("col")
        me = jnp.stack([me_col % 2, (me_col // 2) % 2]).astype(jnp.int32)
        keeps, sends = forward(x_field, u, v, ranks, me, cuts, rb, zs)
        z_me = me_col // 4
        blocks = [observed] + [lax.ppermute(observed, "col", p) for p in z_swaps]
        stacked = jnp.zeros((nz, rb, sources), observed.dtype)
        for k, b in enumerate(blocks):
            stacked = lax.dynamic_update_slice(stacked, b[None], (z_me ^ k, 0, 0))
        obs_t = stacked.reshape(nz * rb, sources).T.astype(F32)
        sat = sat_scale[:, None]

        resid = []
        row = 0
        for i, s in enumerate(cuts):
            got = lax.ppermute(sends[i], "col", core_swap)
            half = keeps[i] + got.astype(F32)
            got = lax.ppermute(half[1].astype(BF), "col", x_swap)
            quarter = half[0] + got.astype(F32)
            mine = quarter.astype(BF)
            total = quarter
            for p in z_swaps:
                total = total + lax.ppermute(mine, "col", p).astype(F32)
            o, sc = obs_t[row : row + s], sat[row : row + s]
            r00 = (sc * jnp.tanh((total - o) / sc)).astype(BF)
            r01 = lax.ppermute(r00, "col", x_swap)
            r10 = lax.ppermute(r00, "col", core_swap)
            r11 = lax.ppermute(r01, "col", core_swap)
            resid.append((r00, r01, r10, r11))
            row += s

        per = tile_cols // GROUPS
        pieces = {}
        for i, s in enumerate(cuts):
            for g in range(GROUPS):
                part = adjoint(resid[i], u, v, ranks, me, g * per, per, rb, zs)
                if n_row == 2:
                    pieces[i, g] = (part, lax.ppermute(part, "row", row_swap))
                else:
                    whole = lax.psum(part.astype(F32), "row").astype(BF)
                    pieces[i, g] = (whole, jnp.zeros_like(whole))
        out = None
        lane = 0
        i = 0
        while i < len(cuts):
            ids, lanes = [i], cuts[i]
            while lanes % 128 != 0:
                ids.append(ids[-1] + 1)
                lanes += cuts[ids[-1]]
            for g in range(GROUPS):
                out = finish(out, [pieces[k, g] for k in ids], g * per, lane // lanes, rows, sources)
            lane += lanes
            i = ids[-1] + 1
        return out

    return jax.shard_map(
        local,
        mesh=mesh,
        in_specs=(
            P("col", None),
            P(("row", "col"), None),
            P(),
            P("row", "col", None, None),
            P("row", "col", None, None),
            P("row", "col"),
        ),
        out_specs=P("col", None),
        check_vma=False,
    )
```

```python
import functools
import math

import jax
import jax.numpy as jnp
from jax import lax
from jax.experimental import pallas as pl
from jax.experimental.pallas import tpu as pltpu
from jax.sharding import PartitionSpec as P


BF = jnp.bfloat16
F32 = jnp.float32
CUTS = (128, 128)
GROUPS = (4, 4)
VMEM_LIMIT = 26 * 2**20
IN_VMEM = pl.BlockSpec(memory_space=pltpu.VMEM)
IN_SMEM = pl.BlockSpec(memory_space=pltpu.SMEM)
IN_HBM = pl.BlockSpec(memory_space=pltpu.HBM)


def dot_nn(a, b):
    return lax.dot_general(a, b, (((1,), (0,)), ((), ())), preferred_element_type=F32)


def dot_nt(a, b):
    return lax.dot_general(a, b, (((1,), (1,)), ((), ())), preferred_element_type=F32)


def permuted_rows(tile, zs, rb):
    return jnp.concatenate(
        [tile[(z * 4 + q) * rb : (z * 4 + q + 1) * rb] for q in range(4) for z in range(zs)], axis=0
    )


def forward_kernel(dims, ranks, me, obs, x_hbm, u_hbm, v_hbm, *rest):
    tile_rows, tile_cols, width, cap, sources, rb, zs, cuts = dims
    n = len(cuts)
    keep_refs, send_refs = rest[:n], rest[n : 2 * n]
    u_vm, v_vm, x_vm, acc, sems = rest[2 * n :]

    def copies(j):
        span = pl.ds(j * width, width)
        yield pltpu.make_async_copy(x_hbm.at[span], x_vm.at[span], sems.at[j, 0])
        for a in range(tile_rows):
            yield pltpu.make_async_copy(v_hbm.at[a, j], v_vm.at[a, j], sems.at[j, 1 + a])
        for a in range(tile_rows):
            yield pltpu.make_async_copy(u_hbm.at[a, j], u_vm.at[a, j], sems.at[j, 1 + tile_rows + a])

    for j in range(tile_cols):
        for c in copies(j):
            c.start()

    mine, my_x, my_z = me[0], me[1], me[2]
    lane = lax.broadcasted_iota(jnp.int32, (sources, cap), 1)
    acc[...] = jnp.zeros_like(acc)

    def body(j, carry):
        for c in copies(j):
            c.wait()
        xt = x_vm[pl.ds(pl.multiple_of(j * width, width), width), :].T
        for a in range(tile_rows):
            c = dot_nn(xt, v_vm[a, j])
            c = jnp.where(lane < ranks[a * tile_cols + j], c, 0.0).astype(BF)
            acc[a] += dot_nt(c, permuted_rows(u_vm[a, j], zs, rb))
        return carry

    lax.fori_loop(0, tile_cols, body, 0)

    nz = zs * tile_rows
    q_lanes = width // 4
    obs_t = obs[...].astype(F32).T
    obs_t = jnp.concatenate([obs_t] * nz, axis=1)
    spot = lax.broadcasted_iota(jnp.int32, (sources, nz * rb), 1)
    obs_t = jnp.where((spot >= my_z * rb) & (spot < (my_z + 1) * rb), obs_t, 0.0)
    for q in range(4):
        qx, qc = q // 2, q % 2
        slot = qx ^ my_x
        row = 0
        for i, s in enumerate(cuts):
            val = jnp.concatenate(
                [acc[a, row : row + s, q * q_lanes : (q + 1) * q_lanes] for a in range(tile_rows)], axis=1
            )

            @pl.when(mine == qc)
            def _():
                own = jnp.where(slot == 0, 1.0, 0.0).astype(F32)
                keep_refs[i][slot] = val - own * obs_t[row : row + s]

            @pl.when(mine != qc)
            def _():
                send_refs[i][slot] = val.astype(BF)

            row += s


def forward(x, obs, u, v, ranks, me, cuts, zs):
    tile_rows, tile_cols, width, cap = u.shape
    sources = x.shape[1]
    rb = obs.shape[0]
    block = tile_rows * width // 4
    dims = (tile_rows, tile_cols, width, cap, sources, rb, zs, cuts)
    outs = [pltpu.VMEM((2, s, block), F32) for s in cuts] + [pltpu.VMEM((2, s, block), BF) for s in cuts]
    outs += [pltpu.VMEM(u.shape, BF), pltpu.VMEM(v.shape, BF)]
    room = 2**20 + sum(math.prod(o.shape) * o.dtype.itemsize for o in outs)
    res = pl.pallas_call(
        functools.partial(forward_kernel, dims),
        in_specs=[IN_SMEM, IN_SMEM, IN_VMEM, IN_HBM, IN_HBM, IN_HBM],
        out_specs=[IN_VMEM] * len(outs),
        scratch_shapes=[
            pltpu.VMEM(x.shape, BF),
            pltpu.VMEM((tile_rows, sources, width), F32),
            pltpu.SemaphoreType.DMA((tile_cols, 1 + 2 * tile_rows)),
        ],
        out_shape=outs,
        compiler_params=pltpu.CompilerParams(vmem_limit_bytes=63 * 2**20 - room),
        cost_estimate=pl.CostEstimate(
            flops=4 * tile_rows * tile_cols * width * cap * sources,
            bytes_accessed=4 * u.size + 2 * x.size,
            transcendentals=0,
        ),
        name="forward",
    )(ranks.reshape(-1), me, obs, x, u, v)
    n = len(cuts)
    return res[:n], res[n : 2 * n], res[2 * n], res[2 * n + 1]


def adjoint_kernel(dims, ranks, me, r00, r01, r10, r11, u_ref, v_ref, g_ref, held):
    tile_rows, tile_cols, start, count, width, cap, s, rb, zs = dims
    base = me[1] * 2 + me[0]
    held[base] = r00[...]
    held[base ^ 2] = r01[...]
    held[base ^ 1] = r10[...]
    held[base ^ 3] = r11[...]
    q_lanes = width // 4
    lane = lax.broadcasted_iota(jnp.int32, (s, cap), 1)
    r = [
        jnp.concatenate([held[q][:, a * q_lanes : (a + 1) * q_lanes] for q in range(4)], axis=1)
        for a in range(tile_rows)
    ]
    for j in range(count):
        total = None
        for a in range(tile_rows):
            adj = dot_nn(r[a], permuted_rows(u_ref[a, start + j], zs, rb))
            adj = jnp.where(lane < ranks[a * tile_cols + start + j], adj, 0.0).astype(BF)
            g = dot_nt(adj, v_ref[a, start + j])
            total = g if total is None else total + g
        g_ref[j] = total.astype(BF)


def adjoint(rs, u, v, ranks, me, start, count, rb, zs):
    tile_rows, tile_cols, width, cap = u.shape
    s, block = rs[0].shape
    dims = (tile_rows, tile_cols, start, count, width, cap, s, rb, zs)
    return pl.pallas_call(
        functools.partial(adjoint_kernel, dims),
        in_specs=[IN_SMEM, IN_SMEM] + [IN_VMEM] * 6,
        out_specs=IN_VMEM,
        scratch_shapes=[pltpu.VMEM((4, s, block), BF)],
        out_shape=jax.ShapeDtypeStruct((count, s, width), BF),
        compiler_params=pltpu.CompilerParams(vmem_limit_bytes=VMEM_LIMIT),
        cost_estimate=pl.CostEstimate(
            flops=4 * tile_rows * count * width * cap * s, bytes_accessed=4 * s * block, transcendentals=0
        ),
        name="adjoint",
    )(ranks.reshape(-1), me, *rs, u, v)


def finish_kernel(n, *refs):
    out = refs[-1]
    j = pl.program_id(0)
    for i in range(n):
        a, b = refs[2 * i], refs[2 * i + 1]
        s = a.shape[1]
        t = a[j].astype(F32) + b[j].astype(F32)
        out[:, i * s : (i + 1) * s] = t.T.astype(BF)


def finish(out, pairs, start, lane_block, rows, sources):
    count, s, width = pairs[0][0].shape
    n = len(pairs)
    flat = [p for pair in pairs for p in pair]
    lanes = n * s
    aliases = {}
    specs = [IN_VMEM] * len(flat)
    body = functools.partial(finish_kernel, n)
    if out is not None:
        aliases = {len(flat): 0}
        specs = specs + [IN_HBM]
        inner, m = body, len(flat)
        body = lambda *refs: inner(*refs[:m], refs[-1])
        flat = flat + [out]
    return pl.pallas_call(
        body,
        grid=(count,),
        in_specs=specs,
        out_specs=pl.BlockSpec((width, lanes), lambda j: (start + j, lane_block)),
        out_shape=jax.ShapeDtypeStruct((rows, sources), BF),
        input_output_aliases=aliases,
        compiler_params=pltpu.CompilerParams(vmem_limit_bytes=VMEM_LIMIT),
        cost_estimate=pl.CostEstimate(flops=0, bytes_accessed=2 * count * lanes * width, transcendentals=0),
        name="finish",
    )(*flat)


def solution(mesh):
    n_row, n_col = mesh.shape["row"], mesh.shape["col"]
    nz = n_col // 4
    assert n_col == 4 * nz and nz & (nz - 1) == 0
    core_swap = [(c, c ^ 1) for c in range(n_col)]
    x_swap = [(c, c ^ 2) for c in range(n_col)]
    z_swaps = [[(c, c ^ (4 * k)) for c in range(n_col)] for k in range(1, nz)]
    row_swap = [(0, 1), (1, 0)]

    def local(x_field, observed, sat_scale, u, v, ranks):
        tile_rows, tile_cols, _, _ = u.shape
        rows, sources = x_field.shape
        rb = observed.shape[0]
        zs = nz // tile_rows
        cuts = tuple(c * sources // 256 for c in CUTS)
        me_col = lax.axis_index("col")
        me = jnp.stack([me_col % 2, (me_col // 2) % 2, me_col // 4]).astype(jnp.int32)
        sat = sat_scale[:, None]
        keeps, sends, u, v = forward(x_field, observed, u, v, ranks, me, cuts, zs)

        def residual(send, keep, sc):
            got = lax.ppermute(send, "col", core_swap)
            half = keep + got.astype(F32)
            got = lax.ppermute(half[1].astype(BF), "col", x_swap)
            quarter = half[0] + got.astype(F32)
            mine = quarter.astype(BF)
            total = quarter
            for p in z_swaps:
                total = total + lax.ppermute(mine, "col", p).astype(F32)
            r00 = (sc * jnp.tanh(total / sc)).astype(BF)
            r01 = lax.ppermute(r00, "col", x_swap)
            r10 = lax.ppermute(r00, "col", core_swap)
            r11 = lax.ppermute(r01, "col", core_swap)
            return r00, r01, r10, r11

        swapped = {}
        row = 0
        for i, s in enumerate(cuts):
            resid = residual(sends[i], keeps[i], sat[row : row + s])
            row += s
            per = tile_cols // GROUPS[i]
            for g in range(GROUPS[i]):
                part = adjoint(resid, u, v, ranks, me, g * per, per, rb, zs)
                if n_row == 2:
                    swapped[i, g] = (part, lax.ppermute(part, "row", row_swap))
                else:
                    whole = lax.psum(part.astype(F32), "row").astype(BF)
                    swapped[i, g] = (whole, jnp.zeros_like(whole))
        out = None
        lane = 0
        i = 0
        while i < len(cuts):
            ids, lanes = [i], cuts[i]
            while lanes % 128 != 0:
                ids.append(ids[-1] + 1)
                lanes += cuts[ids[-1]]
            per = tile_cols // GROUPS[i]
            for g in range(GROUPS[i]):
                out = finish(out, [swapped[k, g] for k in ids], g * per, lane // lanes, rows, sources)
            lane += lanes
            i = ids[-1] + 1
        return out

    return jax.shard_map(
        local,
        mesh=mesh,
        in_specs=(
            P("col", None),
            P(("row", "col"), None),
            P(),
            P("row", "col", None, None),
            P("row", "col", None, None),
            P("row", "col"),
        ),
        out_specs=P("col", None),
        check_vma=False,
    )
```

```python
import functools
import math

import jax
import jax.numpy as jnp
from jax import lax
from jax.experimental import pallas as pl
from jax.experimental.pallas import tpu as pltpu
from jax.sharding import PartitionSpec as P


BF = jnp.bfloat16
F32 = jnp.float32
CUTS = (128, 128)
GROUPS = ((2, 3, 3), (4, 3, 1))
VMEM_LIMIT = 26 * 2**20
IN_VMEM = pl.BlockSpec(memory_space=pltpu.VMEM)
IN_SMEM = pl.BlockSpec(memory_space=pltpu.SMEM)
IN_HBM = pl.BlockSpec(memory_space=pltpu.HBM)


def dot_nn(a, b):
    return lax.dot_general(a, b, (((1,), (0,)), ((), ())), preferred_element_type=F32)


def dot_nt(a, b):
    return lax.dot_general(a, b, (((1,), (1,)), ((), ())), preferred_element_type=F32)


def permuted_rows(tile, zs, rb):
    return jnp.concatenate(
        [tile[(z * 4 + q) * rb : (z * 4 + q + 1) * rb] for q in range(4) for z in range(zs)], axis=0
    )


def position():
    col = lax.axis_index("col")
    return lax.rem(col, 2), lax.rem(lax.div(col, 2), 2), lax.div(col, 4)


def forward_kernel(dims, ranks, obs, x_hbm, u_hbm, v_hbm, *rest):
    tile_rows, tile_cols, width, cap, sources, rb, zs, cuts = dims
    n = len(cuts)
    keep_refs, send_refs = rest[:n], rest[n : 2 * n]
    x_vm, u_vm, v_vm, acc, sems = rest[2 * n :]

    def copies(j):
        span = pl.ds(j * width, width)
        yield pltpu.make_async_copy(x_hbm.at[span], x_vm.at[span], sems.at[j, 0])
        for a in range(tile_rows):
            yield pltpu.make_async_copy(v_hbm.at[a, j], v_vm.at[a, j], sems.at[j, 1 + a])
        for a in range(tile_rows):
            yield pltpu.make_async_copy(u_hbm.at[a, j], u_vm.at[a, j], sems.at[j, 1 + tile_rows + a])

    for j in range(tile_cols):
        for c in copies(j):
            c.start()

    mine, my_x, my_z = position()
    lane = lax.broadcasted_iota(jnp.int32, (sources, cap), 1)
    jb = 2 if tile_cols % 2 == 0 else 1
    for j0 in range(0, tile_cols, jb):
        parts = [[] for _ in range(tile_rows)]
        for j in range(j0, j0 + jb):
            for c in copies(j):
                c.wait()
            xt = x_vm[j * width : (j + 1) * width, :].T
            for a in range(tile_rows):
                c = dot_nn(xt, v_vm[a, j])
                parts[a].append(jnp.where(lane < ranks[a, j], c, 0.0).astype(BF))
        for a in range(tile_rows):
            w = jnp.concatenate([permuted_rows(u_vm[a, j], zs, rb) for j in range(j0, j0 + jb)], axis=1)
            p = dot_nt(jnp.concatenate(parts[a], axis=1), w)
            if j0 == 0:
                acc[a] = p
            else:
                acc[a] += p

    nz = zs * tile_rows
    q_lanes = width // 4
    obs_t = obs[...].astype(F32).T
    obs_t = jnp.concatenate([obs_t] * nz, axis=1)
    spot = lax.broadcasted_iota(jnp.int32, (sources, nz * rb), 1)
    obs_t = jnp.where((spot >= my_z * rb) & (spot < (my_z + 1) * rb), obs_t, 0.0)
    for q in range(4):
        qx, qc = q // 2, q % 2
        slot = qx ^ my_x
        row = 0
        for i, s in enumerate(cuts):
            val = jnp.concatenate(
                [acc[a, row : row + s, q * q_lanes : (q + 1) * q_lanes] for a in range(tile_rows)], axis=1
            )

            @pl.when(mine == qc)
            def _():
                own = jnp.where(slot == 0, 1.0, 0.0).astype(F32)
                keep_refs[i][slot] = val - own * obs_t[row : row + s]

            @pl.when(mine != qc)
            def _():
                send_refs[i][slot] = val.astype(BF)

            row += s


def forward(x, obs, u, v, ranks, cuts, zs):
    tile_rows, tile_cols, width, cap = u.shape
    sources = x.shape[1]
    rb = obs.shape[0]
    block = tile_rows * width // 4
    dims = (tile_rows, tile_cols, width, cap, sources, rb, zs, cuts)
    outs = [pltpu.VMEM((2, s, block), F32) for s in cuts] + [pltpu.VMEM((2, s, block), BF) for s in cuts]
    room = 2**20 + sum(math.prod(o.shape) * o.dtype.itemsize for o in outs)
    res = pl.pallas_call(
        functools.partial(forward_kernel, dims),
        in_specs=[IN_SMEM, IN_VMEM, IN_HBM, IN_HBM, IN_HBM],
        out_specs=[IN_VMEM] * len(outs),
        scratch_shapes=[
            pltpu.VMEM(x.shape, BF),
            pltpu.VMEM(u.shape, BF),
            pltpu.VMEM(v.shape, BF),
            pltpu.VMEM((tile_rows, sources, width), F32),
            pltpu.SemaphoreType.DMA((tile_cols, 1 + 2 * tile_rows)),
        ],
        out_shape=outs,
        compiler_params=pltpu.CompilerParams(vmem_limit_bytes=63 * 2**20 - room),
        cost_estimate=pl.CostEstimate(
            flops=4 * tile_rows * tile_cols * width * cap * sources,
            bytes_accessed=4 * u.size + 2 * x.size,
            transcendentals=0,
        ),
        name="forward",
    )(ranks, obs, x, u, v)
    n = len(cuts)
    return res[:n], res[n:]


def hold_kernel(src, dst, sem):
    copy = pltpu.make_async_copy(src, dst, sem)
    copy.start()
    copy.wait()


def hold(array, before):
    room = before + 2 * array.size + 3 * 2**20
    return pl.pallas_call(
        hold_kernel,
        in_specs=[IN_HBM],
        out_specs=pl.BlockSpec(memory_space=pl.ANY),
        out_shape=pltpu.VMEM(array.shape, array.dtype),
        scratch_shapes=[pltpu.SemaphoreType.DMA],
        compiler_params=pltpu.CompilerParams(vmem_limit_bytes=63 * 2**20 - room),
        cost_estimate=pl.CostEstimate(flops=0, bytes_accessed=2 * array.size, transcendentals=0),
        name="hold",
    )(array)


def adjoint_kernel(dims, ranks, r00, r01, r10, r11, u_ref, v_ref, g_ref, held):
    tile_rows, _, start, count, width, cap, s, rb, zs = dims
    mine, my_x, _ = position()
    base = my_x * 2 + mine
    held[base] = r00[...]
    held[base ^ 2] = r01[...]
    held[base ^ 1] = r10[...]
    held[base ^ 3] = r11[...]
    q_lanes = width // 4
    lane = lax.broadcasted_iota(jnp.int32, (s, cap), 1)
    r = [
        jnp.concatenate([held[q][:, a * q_lanes : (a + 1) * q_lanes] for q in range(4)], axis=1)
        for a in range(tile_rows)
    ]
    for j in range(count):
        total = None
        for a in range(tile_rows):
            adj = dot_nn(r[a], permuted_rows(u_ref[a, start + j], zs, rb))
            adj = jnp.where(lane < ranks[a, start + j], adj, 0.0).astype(BF)
            g = dot_nt(adj, v_ref[a, start + j])
            total = g if total is None else total + g
        g_ref[j] = total.astype(BF)


def adjoint(rs, u, v, ranks, start, count, rb, zs):
    tile_rows, tile_cols, width, cap = u.shape
    s, block = rs[0].shape
    dims = (tile_rows, tile_cols, start, count, width, cap, s, rb, zs)
    return pl.pallas_call(
        functools.partial(adjoint_kernel, dims),
        in_specs=[IN_SMEM] + [IN_VMEM] * 6,
        out_specs=IN_VMEM,
        scratch_shapes=[pltpu.VMEM((4, s, block), BF)],
        out_shape=jax.ShapeDtypeStruct((count, s, width), BF),
        compiler_params=pltpu.CompilerParams(vmem_limit_bytes=VMEM_LIMIT),
        cost_estimate=pl.CostEstimate(
            flops=4 * tile_rows * count * width * cap * s, bytes_accessed=4 * s * block, transcendentals=0
        ),
        name="adjoint",
    )(ranks, *rs, u, v)


def finish_kernel(n, *refs):
    out = refs[-1]
    j = pl.program_id(0)
    for i in range(n):
        a, b = refs[2 * i], refs[2 * i + 1]
        s = a.shape[1]
        t = a[j].astype(F32) + b[j].astype(F32)
        out[:, i * s : (i + 1) * s] = t.T.astype(BF)


def finish(out, pairs, start, lane_block, rows, sources):
    count, s, width = pairs[0][0].shape
    n = len(pairs)
    flat = [p for pair in pairs for p in pair]
    lanes = n * s
    aliases = {}
    specs = [IN_VMEM] * len(flat)
    body = functools.partial(finish_kernel, n)
    if out is not None:
        aliases = {len(flat): 0}
        specs = specs + [IN_HBM]
        inner, m = body, len(flat)
        body = lambda *refs: inner(*refs[:m], refs[-1])
        flat = flat + [out]
    return pl.pallas_call(
        body,
        grid=(count,),
        in_specs=specs,
        out_specs=pl.BlockSpec((width, lanes), lambda j: (start + j, lane_block)),
        out_shape=jax.ShapeDtypeStruct((rows, sources), BF),
        input_output_aliases=aliases,
        compiler_params=pltpu.CompilerParams(vmem_limit_bytes=VMEM_LIMIT),
        cost_estimate=pl.CostEstimate(flops=0, bytes_accessed=2 * count * lanes * width, transcendentals=0),
        name="finish",
    )(*flat)


def solution(mesh):
    n_row, n_col = mesh.shape["row"], mesh.shape["col"]
    nz = n_col // 4
    assert n_col == 4 * nz and nz & (nz - 1) == 0
    core_swap = [(c, c ^ 1) for c in range(n_col)]
    x_swap = [(c, c ^ 2) for c in range(n_col)]
    z_swaps = [[(c, c ^ (4 * k)) for c in range(n_col)] for k in range(1, nz)]
    row_swap = [(0, 1), (1, 0)]

    def local(x_field, observed, sat_scale, u, v, ranks):
        tile_rows, tile_cols, _, _ = u.shape
        rows, sources = x_field.shape
        rb = observed.shape[0]
        zs = nz // tile_rows
        cuts = tuple(c * sources // 256 for c in CUTS)
        sat = sat_scale[:, None]
        keeps, sends = forward(x_field, observed, u, v, ranks, cuts, zs)
        u = hold(u, 0)
        v = hold(v, 2 * u.size)

        def residual(send, keep, sc):
            got = lax.ppermute(send, "col", core_swap)
            half = keep + got.astype(F32)
            got = lax.ppermute(half[1].astype(BF), "col", x_swap)
            quarter = half[0] + got.astype(F32)
            mine = quarter.astype(BF)
            total = quarter
            for p in z_swaps:
                total = total + lax.ppermute(mine, "col", p).astype(F32)
            r00 = (sc * jnp.tanh(total / sc)).astype(BF)
            r01 = lax.ppermute(r00, "col", x_swap)
            r10 = lax.ppermute(r00, "col", core_swap)
            r11 = lax.ppermute(r01, "col", core_swap)
            return r00, r01, r10, r11

        swapped = {}
        row = 0
        for i, s in enumerate(cuts):
            resid = residual(sends[i], keeps[i], sat[row : row + s])
            row += s
            start = 0
            for g, share in enumerate(GROUPS[i]):
                per = share * tile_cols // 8
                part = adjoint(resid, u, v, ranks, start, per, rb, zs)
                start += per
                if n_row == 2:
                    swapped[i, g] = (part, lax.ppermute(part, "row", row_swap))
                else:
                    whole = lax.psum(part.astype(F32), "row").astype(BF)
                    swapped[i, g] = (whole, jnp.zeros_like(whole))
        out = None
        lane = 0
        for i, s in enumerate(cuts):
            start = 0
            for g, share in enumerate(GROUPS[i]):
                out = finish(out, [swapped[i, g]], start, lane // s, rows, sources)
                start += share * tile_cols // 8
            lane += s
        return out

    return jax.shard_map(
        local,
        mesh=mesh,
        in_specs=(
            P("col", None),
            P(("row", "col"), None),
            P(),
            P("row", "col", None, None),
            P("row", "col", None, None),
            P("row", "col"),
        ),
        out_specs=P("col", None),
        check_vma=False,
    )
```

```python
import functools
import math

import jax
import jax.numpy as jnp
from jax import lax
from jax.experimental import pallas as pl
from jax.experimental.pallas import tpu as pltpu
from jax.sharding import PartitionSpec as P


BF = jnp.bfloat16
F32 = jnp.float32
CUTS = (112, 144)
GROUPS = ((3, 5), (4, 3, 1))
VMEM_LIMIT = 26 * 2**20
IN_VMEM = pl.BlockSpec(memory_space=pltpu.VMEM)
IN_SMEM = pl.BlockSpec(memory_space=pltpu.SMEM)
IN_HBM = pl.BlockSpec(memory_space=pltpu.HBM)


def dot_nn(a, b):
    return lax.dot_general(a, b, (((1,), (0,)), ((), ())), preferred_element_type=F32)


def dot_nt(a, b):
    return lax.dot_general(a, b, (((1,), (1,)), ((), ())), preferred_element_type=F32)


def permuted_rows(tile, zs, rb):
    return jnp.concatenate(
        [tile[(z * 4 + q) * rb : (z * 4 + q + 1) * rb] for q in range(4) for z in range(zs)], axis=0
    )


def position():
    col = lax.axis_index("col")
    return lax.rem(col, 2), lax.rem(lax.div(col, 2), 2), lax.div(col, 4)


def forward_kernel(dims, ranks, obs, x_hbm, u_hbm, v_hbm, *rest):
    tile_rows, tile_cols, width, cap, sources, rb, zs, cuts = dims
    n = len(cuts)
    keep_refs, send_refs = rest[:n], rest[n : 2 * n]
    x_vm, u_vm, v_vm, acc, sems = rest[2 * n :]

    def copies(j, first):
        span = pl.ds(j * width, width)
        if first:
            pairs = [(x_hbm.at[span], x_vm.at[span])] + [(v_hbm.at[a, j], v_vm.at[a, j]) for a in range(tile_rows)]
        else:
            pairs = [(u_hbm.at[a, j], u_vm.at[a, j]) for a in range(tile_rows)]
        base = 0 if first else 1 + tile_rows
        return [pltpu.make_async_copy(src, dst, sems.at[j, base + k]) for k, (src, dst) in enumerate(pairs)]

    for j in range(tile_cols):
        for c in copies(j, True) + copies(j, False):
            c.start()

    mine, my_x, my_z = position()
    lane = lax.broadcasted_iota(jnp.int32, (sources, cap), 1)
    jb = 2 if tile_cols % 2 == 0 else 1
    for j0 in range(0, tile_cols, jb):
        parts = [[] for _ in range(tile_rows)]
        for j in range(j0, j0 + jb):
            for c in copies(j, True) + copies(j, False):
                c.wait()
            xt = x_vm[j * width : (j + 1) * width, :].T
            for a in range(tile_rows):
                c = dot_nn(xt, v_vm[a, j])
                parts[a].append(jnp.where(lane < ranks[a, j], c, 0.0).astype(BF))
        for a in range(tile_rows):
            w = jnp.concatenate([permuted_rows(u_vm[a, j], zs, rb) for j in range(j0, j0 + jb)], axis=1)
            p = dot_nt(jnp.concatenate(parts[a], axis=1), w)
            if j0 == 0:
                acc[a] = p
            else:
                acc[a] += p

    nz = zs * tile_rows
    q_lanes = width // 4
    obs_t = obs[...].astype(F32).T
    obs_t = jnp.concatenate([obs_t] * nz, axis=1)
    spot = lax.broadcasted_iota(jnp.int32, (sources, nz * rb), 1)
    obs_t = jnp.where((spot >= my_z * rb) & (spot < (my_z + 1) * rb), obs_t, 0.0)
    for q in range(4):
        qx, qc = q // 2, q % 2
        slot = qx ^ my_x
        row = 0
        for i, s in enumerate(cuts):
            val = jnp.concatenate(
                [acc[a, row : row + s, q * q_lanes : (q + 1) * q_lanes] for a in range(tile_rows)], axis=1
            )

            @pl.when(mine == qc)
            def _():
                own = jnp.where(slot == 0, 1.0, 0.0).astype(F32)
                keep_refs[i][slot] = val - own * obs_t[row : row + s]

            @pl.when(mine != qc)
            def _():
                send_refs[i][slot] = val.astype(BF)

            row += s


def forward(x, obs, u, v, ranks, cuts, zs):
    tile_rows, tile_cols, width, cap = u.shape
    sources = x.shape[1]
    rb = obs.shape[0]
    block = tile_rows * width // 4
    dims = (tile_rows, tile_cols, width, cap, sources, rb, zs, cuts)
    outs = [pltpu.VMEM((2, s, block), F32) for s in cuts] + [pltpu.VMEM((2, s, block), BF) for s in cuts]
    room = 2**20 + sum(math.prod(o.shape) * o.dtype.itemsize for o in outs)
    res = pl.pallas_call(
        functools.partial(forward_kernel, dims),
        in_specs=[IN_SMEM, IN_VMEM, IN_HBM, IN_HBM, IN_HBM],
        out_specs=[IN_VMEM] * len(outs),
        scratch_shapes=[
            pltpu.VMEM(x.shape, BF),
            pltpu.VMEM(u.shape, BF),
            pltpu.VMEM(v.shape, BF),
            pltpu.VMEM((tile_rows, sources, width), F32),
            pltpu.SemaphoreType.DMA((tile_cols, 1 + 2 * tile_rows)),
        ],
        out_shape=outs,
        compiler_params=pltpu.CompilerParams(vmem_limit_bytes=63 * 2**20 - room),
        cost_estimate=pl.CostEstimate(
            flops=4 * tile_rows * tile_cols * width * cap * sources,
            bytes_accessed=4 * u.size + 2 * x.size,
            transcendentals=0,
        ),
        name="forward",
    )(ranks, obs, x, u, v)
    n = len(cuts)
    return res[:n], res[n:]


def hold_kernel(src, dst, sem):
    copy = pltpu.make_async_copy(src, dst, sem)
    copy.start()
    copy.wait()


def hold(array, before):
    room = before + 2 * array.size + 3 * 2**20
    return pl.pallas_call(
        hold_kernel,
        in_specs=[IN_HBM],
        out_specs=pl.BlockSpec(memory_space=pl.ANY),
        out_shape=pltpu.VMEM(array.shape, array.dtype),
        scratch_shapes=[pltpu.SemaphoreType.DMA],
        compiler_params=pltpu.CompilerParams(vmem_limit_bytes=63 * 2**20 - room),
        cost_estimate=pl.CostEstimate(flops=0, bytes_accessed=2 * array.size, transcendentals=0),
        name="hold",
    )(array)


def adjoint_kernel(dims, ranks, r00, r01, r10, r11, u_ref, v_ref, g_ref, held):
    tile_rows, _, start, count, width, cap, s, rb, zs = dims
    mine, my_x, _ = position()
    base = my_x * 2 + mine
    held[base] = r00[...]
    held[base ^ 2] = r01[...]
    held[base ^ 1] = r10[...]
    held[base ^ 3] = r11[...]
    q_lanes = width // 4
    lane = lax.broadcasted_iota(jnp.int32, (s, cap), 1)
    r = [
        jnp.concatenate([held[q][:, a * q_lanes : (a + 1) * q_lanes] for q in range(4)], axis=1)
        for a in range(tile_rows)
    ]
    for j in range(count):
        total = None
        for a in range(tile_rows):
            adj = dot_nn(r[a], permuted_rows(u_ref[a, start + j], zs, rb))
            adj = jnp.where(lane < ranks[a, start + j], adj, 0.0).astype(BF)
            g = dot_nt(adj, v_ref[a, start + j])
            total = g if total is None else total + g
        g_ref[j] = total.astype(BF)


def adjoint(rs, u, v, ranks, start, count, rb, zs):
    tile_rows, tile_cols, width, cap = u.shape
    s, block = rs[0].shape
    dims = (tile_rows, tile_cols, start, count, width, cap, s, rb, zs)
    return pl.pallas_call(
        functools.partial(adjoint_kernel, dims),
        in_specs=[IN_SMEM] + [IN_VMEM] * 6,
        out_specs=IN_VMEM,
        scratch_shapes=[pltpu.VMEM((4, s, block), BF)],
        out_shape=jax.ShapeDtypeStruct((count, s, width), BF),
        compiler_params=pltpu.CompilerParams(vmem_limit_bytes=VMEM_LIMIT),
        cost_estimate=pl.CostEstimate(
            flops=4 * tile_rows * count * width * cap * s, bytes_accessed=4 * s * block, transcendentals=0
        ),
        name="adjoint",
    )(ranks, *rs, u, v)


def finish_kernel(plan, start, *refs):
    buf, sems = refs[-2:]
    out = refs[-3]
    width = buf.shape[1]
    copies = []
    for c, chunks in enumerate(plan):
        t = [refs[2 * k][at].astype(F32) + refs[2 * k + 1][at].astype(F32) for k, at in chunks]
        buf[c] = jnp.concatenate(t, axis=0).astype(BF).T
        copies.append(pltpu.make_async_copy(buf.at[c], out.at[pl.ds((start + c) * width, width)], sems.at[c]))
        copies[-1].start()
    for copy in copies:
        copy.wait()


def finish(out, chunks, start, count, rows, sources):
    flat, index, plan = [], {}, []
    for col in range(start, start + count):
        where = []
        for i, pieces in enumerate(chunks):
            for first, mine, got in pieces:
                if first <= col < first + mine.shape[0]:
                    if (i, first) not in index:
                        index[i, first] = len(flat) // 2
                        flat += [mine, got]
                    where.append((index[i, first], col - first))
        plan.append(where)
    width = flat[0].shape[2]
    specs = [IN_VMEM] * len(flat)
    aliases = {}
    if out is not None:
        aliases = {len(flat): 0}
        specs.append(IN_HBM)
        flat.append(out)
    return pl.pallas_call(
        functools.partial(finish_kernel, plan, start),
        in_specs=specs,
        out_specs=IN_HBM,
        out_shape=jax.ShapeDtypeStruct((rows, sources), BF),
        scratch_shapes=[pltpu.VMEM((count, width, sources), BF), pltpu.SemaphoreType.DMA((count,))],
        input_output_aliases=aliases,
        compiler_params=pltpu.CompilerParams(vmem_limit_bytes=VMEM_LIMIT),
        cost_estimate=pl.CostEstimate(flops=0, bytes_accessed=2 * count * sources * width, transcendentals=0),
        name="finish",
    )(*flat)


def solution(mesh):
    n_row, n_col = mesh.shape["row"], mesh.shape["col"]
    nz = n_col // 4
    assert n_col == 4 * nz and nz & (nz - 1) == 0
    core_swap = [(c, c ^ 1) for c in range(n_col)]
    x_swap = [(c, c ^ 2) for c in range(n_col)]
    z_swaps = [[(c, c ^ (4 * k)) for c in range(n_col)] for k in range(1, nz)]
    row_swap = [(0, 1), (1, 0)]

    def local(x_field, observed, sat_scale, u, v, ranks):
        tile_rows, tile_cols, _, _ = u.shape
        rows, sources = x_field.shape
        rb = observed.shape[0]
        zs = nz // tile_rows
        cuts = tuple(c * sources // 256 for c in CUTS)
        sat = sat_scale[:, None]
        keeps, sends = forward(x_field, observed, u, v, ranks, cuts, zs)
        u = hold(u, 0)
        v = hold(v, 2 * u.size)

        def residual(send, keep, sc):
            got = lax.ppermute(send, "col", core_swap)
            half = keep + got.astype(F32)
            got = lax.ppermute(half[1].astype(BF), "col", x_swap)
            quarter = half[0] + got.astype(F32)
            mine = quarter.astype(BF)
            total = quarter
            for p in z_swaps:
                total = total + lax.ppermute(mine, "col", p).astype(F32)
            r00 = (sc * jnp.tanh(total / sc)).astype(BF)
            r01 = lax.ppermute(r00, "col", x_swap)
            r10 = lax.ppermute(r00, "col", core_swap)
            r11 = lax.ppermute(r01, "col", core_swap)
            return r00, r01, r10, r11

        swapped = [[] for _ in cuts]
        row = 0
        for i, s in enumerate(cuts):
            resid = residual(sends[i], keeps[i], sat[row : row + s])
            row += s
            start = 0
            for share in GROUPS[i]:
                per = share * tile_cols // 8
                part = adjoint(resid, u, v, ranks, start, per, rb, zs)
                if n_row == 2:
                    swapped[i].append((start, part, lax.ppermute(part, "row", row_swap)))
                else:
                    whole = lax.psum(part.astype(F32), "row").astype(BF)
                    swapped[i].append((start, whole, jnp.zeros_like(whole)))
                start += per
        out = None
        for start, part, _ in swapped[-1]:
            out = finish(out, swapped, start, part.shape[0], rows, sources)
        return out

    return jax.shard_map(
        local,
        mesh=mesh,
        in_specs=(
            P("col", None),
            P(("row", "col"), None),
            P(),
            P("row", "col", None, None),
            P("row", "col", None, None),
            P("row", "col"),
        ),
        out_specs=P("col", None),
        check_vma=False,
    )
```

```python
import functools
import math

import jax
import jax.numpy as jnp
from jax import lax
from jax.experimental import pallas as pl
from jax.experimental.pallas import tpu as pltpu
from jax.sharding import PartitionSpec as P


BF = jnp.bfloat16
F32 = jnp.float32
CUTS = (144, 112)
GROUPS = ((3, 3), (3, 2, 1))
VMEM_LIMIT = 26 * 2**20
IN_VMEM = pl.BlockSpec(memory_space=pltpu.VMEM)
IN_SMEM = pl.BlockSpec(memory_space=pltpu.SMEM)
IN_HBM = pl.BlockSpec(memory_space=pltpu.HBM)


def dot_nn(a, b):
    return lax.dot_general(a, b, (((1,), (0,)), ((), ())), preferred_element_type=F32)


def dot_nt(a, b):
    return lax.dot_general(a, b, (((1,), (1,)), ((), ())), preferred_element_type=F32)


def permuted_rows(tile, zs, rb):
    return jnp.concatenate(
        [tile[(z * 4 + q) * rb : (z * 4 + q + 1) * rb] for q in range(4) for z in range(zs)], axis=0
    )


def position():
    col = lax.axis_index("col")
    return lax.rem(col, 2), lax.rem(lax.div(col, 2), 2), lax.div(col, 4)


def forward_kernel(dims, ranks, obs, x_hbm, u_hbm, v_hbm, *rest):
    tile_rows, tile_cols, width, cap, sources, rb, zs, cuts, shared = dims
    n = len(cuts)
    keep_refs, send_refs = rest[:n], rest[n : 2 * n]
    x_vm, u_vm, v_vm, acc, sems = rest[-5:]

    def copies(j, first):
        span = pl.ds(j * width, width)
        if first:
            pairs = [(x_hbm.at[span], x_vm.at[span])] + [(v_hbm.at[a, j], v_vm.at[a, j]) for a in range(tile_rows)]
        else:
            pairs = [(u_hbm.at[a, j], u_vm.at[a, j]) for a in range(tile_rows)]
        base = 0 if first else 1 + tile_rows
        return [pltpu.make_async_copy(src, dst, sems.at[j, base + k]) for k, (src, dst) in enumerate(pairs)]

    jb = 2 if tile_cols % 2 == 0 else 1
    steps = list(range(0, tile_cols, jb))[::-1]
    for j0 in steps:
        for j in range(j0, j0 + jb):
            for c in copies(j, True) + copies(j, False):
                c.start()

    mine, my_x, my_z = position()
    lane = lax.broadcasted_iota(jnp.int32, (sources, cap), 1)
    early_copies = []
    for j0 in steps:
        parts = [[] for _ in range(tile_rows)]
        for j in range(j0, j0 + jb):
            for c in copies(j, True) + copies(j, False):
                c.wait()
            xt = x_vm[j * width : (j + 1) * width, :].T
            for a in range(tile_rows):
                c = dot_nn(xt, v_vm[a, j])
                parts[a].append(jnp.where(lane < ranks[a, j], c, 0.0).astype(BF))
        for a in range(tile_rows):
            w = jnp.concatenate([permuted_rows(u_vm[a, j], zs, rb) for j in range(j0, j0 + jb)], axis=1)
            p = dot_nt(jnp.concatenate(parts[a], axis=1), w)
            if j0 == steps[0]:
                acc[a] = p
            else:
                acc[a] += p
        if shared and j0 == steps[0]:
            early, masked, early_sems = rest[2 * n : 2 * n + 3]
            col = tile_cols - 1 - lax.axis_index("row")
            rank_lane = lax.broadcasted_iota(jnp.int32, (width, cap), 1)
            for a in range(tile_rows):
                masked[a] = jnp.where(rank_lane < ranks[a, col], u_vm[a, col], jnp.zeros((), BF))
                early_copies.append(pltpu.make_async_copy(masked.at[a], early.at[0, a], early_sems.at[0, a]))
                early_copies.append(pltpu.make_async_copy(v_vm.at[a, col], early.at[1, a], early_sems.at[1, a]))
            for c in early_copies:
                c.start()

    nz = zs * tile_rows
    q_lanes = width // 4
    obs_t = obs[...].astype(F32).T
    obs_t = jnp.concatenate([obs_t] * nz, axis=1)
    spot = lax.broadcasted_iota(jnp.int32, (sources, nz * rb), 1)
    obs_t = jnp.where((spot >= my_z * rb) & (spot < (my_z + 1) * rb), obs_t, 0.0)
    for q in range(4):
        qx, qc = q // 2, q % 2
        slot = qx ^ my_x
        row = 0
        for i, s in enumerate(cuts):
            val = jnp.concatenate(
                [acc[a, row : row + s, q * q_lanes : (q + 1) * q_lanes] for a in range(tile_rows)], axis=1
            )

            @pl.when(mine == qc)
            def _():
                own = jnp.where(slot == 0, 1.0, 0.0).astype(F32)
                keep_refs[i][slot] = val - own * obs_t[row : row + s]

            @pl.when(mine != qc)
            def _():
                send_refs[i][slot] = val.astype(BF)

            row += s
    for c in early_copies:
        c.wait()


def forward(x, obs, u, v, ranks, cuts, zs, shared):
    tile_rows, tile_cols, width, cap = u.shape
    sources = x.shape[1]
    rb = obs.shape[0]
    block = tile_rows * width // 4
    dims = (tile_rows, tile_cols, width, cap, sources, rb, zs, cuts, shared)
    outs = [pltpu.VMEM((2, s, block), F32) for s in cuts] + [pltpu.VMEM((2, s, block), BF) for s in cuts]
    out_specs = [IN_VMEM] * len(outs)
    extra = []
    if shared:
        outs.append(pltpu.VMEM((2, tile_rows, width, cap), BF))
        out_specs.append(pl.BlockSpec(memory_space=pl.ANY))
        extra = [pltpu.VMEM((tile_rows, width, cap), BF), pltpu.SemaphoreType.DMA((2, tile_rows))]
    room = 2**20 + sum(math.prod(o.shape) * o.dtype.itemsize for o in outs)
    res = pl.pallas_call(
        functools.partial(forward_kernel, dims),
        in_specs=[IN_SMEM, IN_VMEM, IN_HBM, IN_HBM, IN_HBM],
        out_specs=out_specs,
        scratch_shapes=extra
        + [
            pltpu.VMEM(x.shape, BF),
            pltpu.VMEM(u.shape, BF),
            pltpu.VMEM(v.shape, BF),
            pltpu.VMEM((tile_rows, sources, width), F32),
            pltpu.SemaphoreType.DMA((tile_cols, 1 + 2 * tile_rows)),
        ],
        out_shape=outs,
        compiler_params=pltpu.CompilerParams(vmem_limit_bytes=63 * 2**20 - room),
        cost_estimate=pl.CostEstimate(
            flops=4 * tile_rows * tile_cols * width * cap * sources,
            bytes_accessed=4 * u.size + 2 * x.size,
            transcendentals=0,
        ),
        name="forward",
    )(ranks, obs, x, u, v)
    n = len(cuts)
    return res[:n], res[n : 2 * n], res[2 * n :]


def hold_kernel(src, dst, sem):
    copy = pltpu.make_async_copy(src, dst, sem)
    copy.start()
    copy.wait()


def hold(array, before):
    room = before + 2 * array.size + 3 * 2**20
    return pl.pallas_call(
        hold_kernel,
        in_specs=[IN_HBM],
        out_specs=pl.BlockSpec(memory_space=pl.ANY),
        out_shape=pltpu.VMEM(array.shape, array.dtype),
        scratch_shapes=[pltpu.SemaphoreType.DMA],
        compiler_params=pltpu.CompilerParams(vmem_limit_bytes=63 * 2**20 - room),
        cost_estimate=pl.CostEstimate(flops=0, bytes_accessed=2 * array.size, transcendentals=0),
        name="hold",
    )(array)


def adjoint_kernel(dims, ranks, r00, r01, r10, r11, u_ref, v_ref, g_ref, held):
    tile_rows, _, start, count, width, cap, s, rb, zs = dims
    mine, my_x, _ = position()
    base = my_x * 2 + mine
    held[base] = r00[...]
    held[base ^ 2] = r01[...]
    held[base ^ 1] = r10[...]
    held[base ^ 3] = r11[...]
    q_lanes = width // 4
    lane = lax.broadcasted_iota(jnp.int32, (s, cap), 1)
    r = [
        jnp.concatenate([held[q][:, a * q_lanes : (a + 1) * q_lanes] for q in range(4)], axis=1)
        for a in range(tile_rows)
    ]
    for j in range(count):
        total = None
        for a in range(tile_rows):
            adj = dot_nn(r[a], permuted_rows(u_ref[a, start + j], zs, rb))
            adj = jnp.where(lane < ranks[a, start + j], adj, 0.0).astype(BF)
            g = dot_nt(adj, v_ref[a, start + j])
            total = g if total is None else total + g
        g_ref[j] = total.astype(BF)


def adjoint(rs, u, v, ranks, start, count, rb, zs):
    tile_rows, tile_cols, width, cap = u.shape
    s, block = rs[0].shape
    dims = (tile_rows, tile_cols, start, count, width, cap, s, rb, zs)
    return pl.pallas_call(
        functools.partial(adjoint_kernel, dims),
        in_specs=[IN_SMEM] + [IN_VMEM] * 6,
        out_specs=IN_VMEM,
        scratch_shapes=[pltpu.VMEM((4, s, block), BF)],
        out_shape=jax.ShapeDtypeStruct((count, s, width), BF),
        compiler_params=pltpu.CompilerParams(vmem_limit_bytes=VMEM_LIMIT),
        cost_estimate=pl.CostEstimate(
            flops=4 * tile_rows * count * width * cap * s, bytes_accessed=4 * s * block, transcendentals=0
        ),
        name="adjoint",
    )(ranks, *rs, u, v)


def pair_kernel(dims, ranks, *refs):
    tile_rows, tile_cols, width, cap, cuts, rb, zs = dims
    n = len(cuts)
    other = refs[4 * n : 4 * n + 4]
    got, u_ref, v_ref, g_ref, held, theirs = refs[4 * n + 4 :]
    mine, my_x, _ = position()
    base = my_x * 2 + mine
    for k, bits in enumerate((0, 2, 1, 3)):
        row = 0
        for i, s in enumerate(cuts):
            held[base ^ bits, row : row + s] = refs[4 * i + k][...]
            row += s
        theirs[base ^ bits] = other[k][...]
    col = tile_cols - 2 + lax.axis_index("row")
    q_lanes = width // 4
    sources = held.shape[1]
    lane = lax.broadcasted_iota(jnp.int32, (sources, cap), 1)
    total = None
    for a in range(tile_rows):
        span = slice(a * q_lanes, (a + 1) * q_lanes)
        r = jnp.concatenate([held[q][:, span] for q in range(4)], axis=1)
        adj = dot_nn(r, permuted_rows(u_ref[a, col], zs, rb))
        adj = jnp.where(lane < ranks[a, col], adj, 0.0).astype(BF)
        g = dot_nt(adj, v_ref[a, col])
        total = g if total is None else total + g
        r = jnp.concatenate([theirs[q][:, span] for q in range(4)], axis=1)
        adj = dot_nn(r, permuted_rows(got[0, a], zs, rb)).astype(BF)
        total = total + dot_nt(adj, got[1, a])
    g_ref[...] = total.astype(BF)


def pair_column(resid, other, got, u, v, ranks, rb, zs):
    tile_rows, tile_cols, width, cap = u.shape
    cuts = tuple(rs[0].shape[0] for rs in resid)
    sources, block = other[0].shape
    dims = (tile_rows, tile_cols, width, cap, cuts, rb, zs)
    flat = [r for rs in resid for r in rs] + list(other)
    return pl.pallas_call(
        functools.partial(pair_kernel, dims),
        in_specs=[IN_SMEM] + [IN_VMEM] * (len(flat) + 3),
        out_specs=IN_VMEM,
        scratch_shapes=[pltpu.VMEM((4, sources, block), BF)] * 2,
        out_shape=pltpu.VMEM((sources, width), BF),
        compiler_params=pltpu.CompilerParams(vmem_limit_bytes=VMEM_LIMIT),
        cost_estimate=pl.CostEstimate(
            flops=8 * tile_rows * width * cap * sources, bytes_accessed=4 * sources * block, transcendentals=0
        ),
        name="pair",
    )(ranks, *flat, got, u, v)


def join_kernel(*refs):
    row = 0
    for r in refs[:-1]:
        refs[-1][row : row + r.shape[0]] = r[...]
        row += r.shape[0]


def join(parts):
    shape = (sum(p.shape[0] for p in parts), parts[0].shape[1])
    return pl.pallas_call(
        join_kernel,
        in_specs=[IN_VMEM] * len(parts),
        out_specs=IN_VMEM,
        out_shape=pltpu.VMEM(shape, BF),
        compiler_params=pltpu.CompilerParams(vmem_limit_bytes=VMEM_LIMIT),
        cost_estimate=pl.CostEstimate(flops=0, bytes_accessed=4 * shape[0] * shape[1], transcendentals=0),
        name="join",
    )(*parts)


def place_kernel(tile_cols, flip, g_ref, _, out, buf, sem):
    row = lax.axis_index("row")
    width = buf.shape[0]
    col = tile_cols - 2 + (1 - row if flip else row)
    buf[...] = g_ref[...].T
    copy = pltpu.make_async_copy(buf, out.at[pl.ds(pl.multiple_of(col * width, width), width)], sem)
    copy.start()
    copy.wait()


def place(out, column, tile_cols, flip):
    sources, width = column.shape
    return pl.pallas_call(
        functools.partial(place_kernel, tile_cols, flip),
        in_specs=[IN_VMEM, IN_HBM],
        out_specs=IN_HBM,
        out_shape=jax.ShapeDtypeStruct(out.shape, BF),
        scratch_shapes=[pltpu.VMEM((width, sources), BF), pltpu.SemaphoreType.DMA],
        input_output_aliases={1: 0},
        compiler_params=pltpu.CompilerParams(vmem_limit_bytes=VMEM_LIMIT),
        cost_estimate=pl.CostEstimate(flops=0, bytes_accessed=2 * sources * width, transcendentals=0),
        name="place",
    )(column, out)


def finish_kernel(plan, start, *refs):
    buf, sems = refs[-2:]
    out = refs[-3]
    width = buf.shape[1]
    copies = []
    for c, chunks in enumerate(plan):
        t = [refs[2 * k][at].astype(F32) + refs[2 * k + 1][at].astype(F32) for k, at in chunks]
        buf[c] = jnp.concatenate(t, axis=0).astype(BF).T
        copies.append(pltpu.make_async_copy(buf.at[c], out.at[pl.ds((start + c) * width, width)], sems.at[c]))
        copies[-1].start()
    for copy in copies:
        copy.wait()


def finish(out, chunks, start, count, rows, sources):
    flat, index, plan = [], {}, []
    for col in range(start, start + count):
        where = []
        for i, pieces in enumerate(chunks):
            for first, mine, got in pieces:
                if first <= col < first + mine.shape[0]:
                    if (i, first) not in index:
                        index[i, first] = len(flat) // 2
                        flat += [mine, got]
                    where.append((index[i, first], col - first))
        plan.append(where)
    width = flat[0].shape[2]
    specs = [IN_VMEM] * len(flat)
    aliases = {}
    if out is not None:
        aliases = {len(flat): 0}
        specs.append(IN_HBM)
        flat.append(out)
    return pl.pallas_call(
        functools.partial(finish_kernel, plan, start),
        in_specs=specs,
        out_specs=IN_HBM,
        out_shape=jax.ShapeDtypeStruct((rows, sources), BF),
        scratch_shapes=[pltpu.VMEM((count, width, sources), BF), pltpu.SemaphoreType.DMA((count,))],
        input_output_aliases=aliases,
        compiler_params=pltpu.CompilerParams(vmem_limit_bytes=VMEM_LIMIT),
        cost_estimate=pl.CostEstimate(flops=0, bytes_accessed=2 * count * sources * width, transcendentals=0),
        name="finish",
    )(*flat)


def solution(mesh):
    n_row, n_col = mesh.shape["row"], mesh.shape["col"]
    nz = n_col // 4
    assert n_col == 4 * nz and nz & (nz - 1) == 0
    core_swap = [(c, c ^ 1) for c in range(n_col)]
    x_swap = [(c, c ^ 2) for c in range(n_col)]
    z_swaps = [[(c, c ^ (4 * k)) for c in range(n_col)] for k in range(1, nz)]
    row_swap = [(0, 1), (1, 0)]

    def local(x_field, observed, sat_scale, u, v, ranks):
        tile_rows, tile_cols, _, _ = u.shape
        rows, sources = x_field.shape
        rb = observed.shape[0]
        zs = nz // tile_rows
        cuts = tuple(c * sources // 256 for c in CUTS)
        sat = sat_scale[:, None]
        shared = n_row == 2
        keeps, sends, early = forward(x_field, observed, u, v, ranks, cuts, zs, shared)
        cols = tile_cols - 2 if shared else tile_cols
        if shared:
            theirs = lax.ppermute(early[0], "row", row_swap)
        u = hold(u, 0)
        v = hold(v, 2 * u.size)

        def residual(send, keep, sc):
            got = lax.ppermute(send, "col", core_swap)
            half = keep + got.astype(F32)
            got = lax.ppermute(half[1].astype(BF), "col", x_swap)
            quarter = half[0] + got.astype(F32)
            mine = quarter.astype(BF)
            total = quarter
            for p in z_swaps:
                total = total + lax.ppermute(mine, "col", p).astype(F32)
            r00 = (sc * jnp.tanh(total / sc)).astype(BF)
            r01 = lax.ppermute(r00, "col", x_swap)
            if shared:
                other.append(lax.ppermute(r00, "row", row_swap))
            return (r00, r01) + gather(r00, r01)

        def gather(r00, r01):
            return lax.ppermute(r00, "col", core_swap), lax.ppermute(r01, "col", core_swap)

        swapped = [[] for _ in cuts]
        resids, other = [], []
        row = 0
        for i, s in enumerate(cuts):
            resid = residual(sends[i], keeps[i], sat[row : row + s])
            resids.append(resid)
            row += s
            start = 0
            for g in range(len(GROUPS[i])):
                per = sum(GROUPS[i][: g + 1]) * cols // sum(GROUPS[i]) - start
                part = adjoint(resid, u, v, ranks, start, per, rb, zs)
                if n_row == 2:
                    swapped[i].append((start, part, lax.ppermute(part, "row", row_swap)))
                else:
                    whole = lax.psum(part.astype(F32), "row").astype(BF)
                    swapped[i].append((start, whole, jnp.zeros_like(whole)))
                start += per
        if shared:
            r00 = join(other)
            r01 = lax.ppermute(r00, "col", x_swap)
            blocks = (r00, r01) + gather(r00, r01)
            column = pair_column(resids, blocks, theirs, u, v, ranks, rb, zs)
            column_got = lax.ppermute(column, "row", row_swap)
        out = None
        for start, part, _ in swapped[-1]:
            out = finish(out, swapped, start, part.shape[0], rows, sources)
        if shared:
            out = place(out, column, tile_cols, False)
            out = place(out, column_got, tile_cols, True)
        return out

    return jax.shard_map(
        local,
        mesh=mesh,
        in_specs=(
            P("col", None),
            P(("row", "col"), None),
            P(),
            P("row", "col", None, None),
            P("row", "col", None, None),
            P("row", "col"),
        ),
        out_specs=P("col", None),
        check_vma=False,
    )
```

```python
import functools
import math

import jax
import jax.numpy as jnp
from jax import lax
from jax.experimental import pallas as pl
from jax.experimental.pallas import tpu as pltpu
from jax.sharding import PartitionSpec as P


BF = jnp.bfloat16
F32 = jnp.float32
CUTS = (128, 128)
GROUPS = ((3, 3), (3, 3))
VMEM_LIMIT = 26 * 2**20
IN_VMEM = pl.BlockSpec(memory_space=pltpu.VMEM)
IN_SMEM = pl.BlockSpec(memory_space=pltpu.SMEM)
IN_HBM = pl.BlockSpec(memory_space=pltpu.HBM)


def dot_nn(a, b):
    return lax.dot_general(a, b, (((1,), (0,)), ((), ())), preferred_element_type=F32)


def dot_nt(a, b):
    return lax.dot_general(a, b, (((1,), (1,)), ((), ())), preferred_element_type=F32)


def permuted_rows(tile, zs, rb):
    return jnp.concatenate(
        [tile[(z * 4 + q) * rb : (z * 4 + q + 1) * rb] for q in range(4) for z in range(zs)], axis=0
    )


def position():
    col = lax.axis_index("col")
    return lax.rem(col, 2), lax.rem(lax.div(col, 2), 2), lax.div(col, 4)


def forward_kernel(dims, ranks, obs, x_hbm, u_hbm, v_hbm, *rest):
    tile_rows, tile_cols, width, cap, sources, rb, zs, cuts, shared = dims
    n = len(cuts)
    keep_refs, send_refs = rest[:n], rest[n : 2 * n]
    x_vm, u_vm, v_vm, acc, sems = rest[-5:]

    def copies(j, first):
        span = pl.ds(j * width, width)
        if first:
            pairs = [(x_hbm.at[span], x_vm.at[span])] + [(v_hbm.at[a, j], v_vm.at[a, j]) for a in range(tile_rows)]
        else:
            pairs = [(u_hbm.at[a, j], u_vm.at[a, j]) for a in range(tile_rows)]
        base = 0 if first else 1 + tile_rows
        return [pltpu.make_async_copy(src, dst, sems.at[j, base + k]) for k, (src, dst) in enumerate(pairs)]

    jb = 2 if tile_cols % 2 == 0 else 1
    steps = [tuple(range(j, j + jb)) for j in range(0, tile_cols, jb)][::-1]
    if jb == 2:
        steps[-1:] = [(1,), (0,)]
    for step in steps:
        for j in step:
            for c in copies(j, True) + copies(j, False):
                c.start()

    mine, my_x, my_z = position()
    lane = lax.broadcasted_iota(jnp.int32, (sources, cap), 1)
    early_copies = []
    last = []
    for step in steps:
        parts = [[] for _ in range(tile_rows)]
        for j in step:
            for c in copies(j, True) + copies(j, False):
                c.wait()
            xt = x_vm[j * width : (j + 1) * width, :].T
            for a in range(tile_rows):
                c = dot_nn(xt, v_vm[a, j])
                parts[a].append(jnp.where(lane < ranks[a, j], c, 0.0).astype(BF))
        for a in range(tile_rows):
            w = jnp.concatenate([permuted_rows(u_vm[a, j], zs, rb) for j in step], axis=1)
            p = dot_nt(jnp.concatenate(parts[a], axis=1), w)
            if step == steps[0]:
                acc[a] = p
            elif step == steps[-1]:
                last.append(p)
            else:
                acc[a] += p
        if shared and step == steps[0]:
            early, masked, early_sems = rest[2 * n : 2 * n + 3]
            col = tile_cols - 1 - lax.axis_index("row")
            rank_lane = lax.broadcasted_iota(jnp.int32, (width, cap), 1)
            for a in range(tile_rows):
                masked[a] = jnp.where(rank_lane < ranks[a, col], u_vm[a, col], jnp.zeros((), BF))
                early_copies.append(pltpu.make_async_copy(masked.at[a], early.at[0, a], early_sems.at[0, a]))
                early_copies.append(pltpu.make_async_copy(v_vm.at[a, col], early.at[1, a], early_sems.at[1, a]))
            for c in early_copies:
                c.start()

    nz = zs * tile_rows
    q_lanes = width // 4
    obs_t = obs[...].astype(F32).T
    obs_t = jnp.concatenate([obs_t] * nz, axis=1)
    spot = lax.broadcasted_iota(jnp.int32, (sources, nz * rb), 1)
    obs_t = jnp.where((spot >= my_z * rb) & (spot < (my_z + 1) * rb), obs_t, 0.0)
    for q in range(4):
        qx, qc = q // 2, q % 2
        slot = qx ^ my_x
        row = 0
        for i, s in enumerate(cuts):
            val = jnp.concatenate(
                [
                    acc[a, row : row + s, q * q_lanes : (q + 1) * q_lanes]
                    + last[a][row : row + s, q * q_lanes : (q + 1) * q_lanes]
                    for a in range(tile_rows)
                ],
                axis=1,
            )

            @pl.when(mine == qc)
            def _():
                own = jnp.where(slot == 0, 1.0, 0.0).astype(F32)
                keep_refs[i][slot] = val - own * obs_t[row : row + s]

            @pl.when(mine != qc)
            def _():
                send_refs[i][slot] = val.astype(BF)

            row += s
    for c in early_copies:
        c.wait()


def forward(x, obs, u, v, ranks, cuts, zs, shared):
    tile_rows, tile_cols, width, cap = u.shape
    sources = x.shape[1]
    rb = obs.shape[0]
    block = tile_rows * width // 4
    dims = (tile_rows, tile_cols, width, cap, sources, rb, zs, cuts, shared)
    outs = [pltpu.VMEM((2, s, block), F32) for s in cuts] + [pltpu.VMEM((2, s, block), BF) for s in cuts]
    out_specs = [IN_VMEM] * len(outs)
    extra = []
    if shared:
        outs.append(pltpu.VMEM((2, tile_rows, width, cap), BF))
        out_specs.append(pl.BlockSpec(memory_space=pl.ANY))
        extra = [pltpu.VMEM((tile_rows, width, cap), BF), pltpu.SemaphoreType.DMA((2, tile_rows))]
    room = 2**20 + sum(math.prod(o.shape) * o.dtype.itemsize for o in outs)
    res = pl.pallas_call(
        functools.partial(forward_kernel, dims),
        in_specs=[IN_SMEM, IN_VMEM, IN_HBM, IN_HBM, IN_HBM],
        out_specs=out_specs,
        scratch_shapes=extra
        + [
            pltpu.VMEM(x.shape, BF),
            pltpu.VMEM(u.shape, BF),
            pltpu.VMEM(v.shape, BF),
            pltpu.VMEM((tile_rows, sources, width), F32),
            pltpu.SemaphoreType.DMA((tile_cols, 1 + 2 * tile_rows)),
        ],
        out_shape=outs,
        compiler_params=pltpu.CompilerParams(vmem_limit_bytes=63 * 2**20 - room),
        cost_estimate=pl.CostEstimate(
            flops=4 * tile_rows * tile_cols * width * cap * sources,
            bytes_accessed=4 * u.size + 2 * x.size,
            transcendentals=0,
        ),
        name="forward",
    )(ranks, obs, x, u, v)
    n = len(cuts)
    return res[:n], res[n : 2 * n], res[2 * n :]


def hold_kernel(src, dst, sem):
    copy = pltpu.make_async_copy(src, dst, sem)
    copy.start()
    copy.wait()


def hold(array, before):
    room = before + 2 * array.size + 3 * 2**20
    return pl.pallas_call(
        hold_kernel,
        in_specs=[IN_HBM],
        out_specs=pl.BlockSpec(memory_space=pl.ANY),
        out_shape=pltpu.VMEM(array.shape, array.dtype),
        scratch_shapes=[pltpu.SemaphoreType.DMA],
        compiler_params=pltpu.CompilerParams(vmem_limit_bytes=63 * 2**20 - room),
        cost_estimate=pl.CostEstimate(flops=0, bytes_accessed=2 * array.size, transcendentals=0),
        name="hold",
    )(array)


def adjoint_kernel(dims, ranks, r00, r01, r10, r11, u_ref, v_ref, g_ref, held):
    tile_rows, _, start, count, width, cap, s, rb, zs = dims
    mine, my_x, _ = position()
    base = my_x * 2 + mine
    held[base] = r00[...]
    held[base ^ 2] = r01[...]
    held[base ^ 1] = r10[...]
    held[base ^ 3] = r11[...]
    q_lanes = width // 4
    lane = lax.broadcasted_iota(jnp.int32, (s, cap), 1)
    r = [
        jnp.concatenate([held[q][:, a * q_lanes : (a + 1) * q_lanes] for q in range(4)], axis=1)
        for a in range(tile_rows)
    ]
    for j in range(count):
        total = None
        for a in range(tile_rows):
            adj = dot_nn(r[a], permuted_rows(u_ref[a, start + j], zs, rb))
            adj = jnp.where(lane < ranks[a, start + j], adj, 0.0).astype(BF)
            g = dot_nt(adj, v_ref[a, start + j])
            total = g if total is None else total + g
        g_ref[j] = total.astype(BF)


def adjoint(rs, u, v, ranks, start, count, rb, zs):
    tile_rows, tile_cols, width, cap = u.shape
    s, block = rs[0].shape
    dims = (tile_rows, tile_cols, start, count, width, cap, s, rb, zs)
    return pl.pallas_call(
        functools.partial(adjoint_kernel, dims),
        in_specs=[IN_SMEM] + [IN_VMEM] * 6,
        out_specs=IN_VMEM,
        scratch_shapes=[pltpu.VMEM((4, s, block), BF)],
        out_shape=jax.ShapeDtypeStruct((count, s, width), BF),
        compiler_params=pltpu.CompilerParams(vmem_limit_bytes=VMEM_LIMIT),
        cost_estimate=pl.CostEstimate(
            flops=4 * tile_rows * count * width * cap * s, bytes_accessed=4 * s * block, transcendentals=0
        ),
        name="adjoint",
    )(ranks, *rs, u, v)


def pair_kernel(dims, ranks, *refs):
    tile_rows, tile_cols, width, cap, cuts, rb, zs = dims
    n = len(cuts)
    other = refs[4 * n : 4 * n + 4]
    got, u_ref, v_ref, g_ref, held, theirs = refs[4 * n + 4 :]
    mine, my_x, _ = position()
    base = my_x * 2 + mine
    for k, bits in enumerate((0, 2, 1, 3)):
        row = 0
        for i, s in enumerate(cuts):
            held[base ^ bits, row : row + s] = refs[4 * i + k][...]
            row += s
        theirs[base ^ bits] = other[k][...]
    col = tile_cols - 2 + lax.axis_index("row")
    q_lanes = width // 4
    sources = held.shape[1]
    lane = lax.broadcasted_iota(jnp.int32, (sources, cap), 1)
    total = None
    for a in range(tile_rows):
        span = slice(a * q_lanes, (a + 1) * q_lanes)
        r = jnp.concatenate([held[q][:, span] for q in range(4)], axis=1)
        adj = dot_nn(r, permuted_rows(u_ref[a, col], zs, rb))
        adj = jnp.where(lane < ranks[a, col], adj, 0.0).astype(BF)
        g = dot_nt(adj, v_ref[a, col])
        total = g if total is None else total + g
        r = jnp.concatenate([theirs[q][:, span] for q in range(4)], axis=1)
        adj = dot_nn(r, permuted_rows(got[0, a], zs, rb)).astype(BF)
        total = total + dot_nt(adj, got[1, a])
    g_ref[...] = total.astype(BF)


def pair_column(resid, other, got, u, v, ranks, rb, zs):
    tile_rows, tile_cols, width, cap = u.shape
    cuts = tuple(rs[0].shape[0] for rs in resid)
    sources, block = other[0].shape
    dims = (tile_rows, tile_cols, width, cap, cuts, rb, zs)
    flat = [r for rs in resid for r in rs] + list(other)
    return pl.pallas_call(
        functools.partial(pair_kernel, dims),
        in_specs=[IN_SMEM] + [IN_VMEM] * (len(flat) + 3),
        out_specs=IN_VMEM,
        scratch_shapes=[pltpu.VMEM((4, sources, block), BF)] * 2,
        out_shape=pltpu.VMEM((sources, width), BF),
        compiler_params=pltpu.CompilerParams(vmem_limit_bytes=VMEM_LIMIT),
        cost_estimate=pl.CostEstimate(
            flops=8 * tile_rows * width * cap * sources, bytes_accessed=4 * sources * block, transcendentals=0
        ),
        name="pair",
    )(ranks, *flat, got, u, v)


def join_kernel(*refs):
    row = 0
    for r in refs[:-1]:
        refs[-1][row : row + r.shape[0]] = r[...]
        row += r.shape[0]


def join(parts):
    shape = (sum(p.shape[0] for p in parts), parts[0].shape[1])
    return pl.pallas_call(
        join_kernel,
        in_specs=[IN_VMEM] * len(parts),
        out_specs=IN_VMEM,
        out_shape=pltpu.VMEM(shape, BF),
        compiler_params=pltpu.CompilerParams(vmem_limit_bytes=VMEM_LIMIT),
        cost_estimate=pl.CostEstimate(flops=0, bytes_accessed=4 * shape[0] * shape[1], transcendentals=0),
        name="join",
    )(*parts)


def interleave_kernel(cuts, own, rest, out):
    odd = lax.rem(lax.div(lax.axis_index("col"), 4), 2)
    row = 0
    for s in cuts:
        half = s // 2
        span = slice(row // 2, row // 2 + half)
        out[pl.ds(pl.multiple_of(row + odd * half, 16), half)] = own[span]
        out[pl.ds(pl.multiple_of(row + (1 - odd) * half, 16), half)] = rest[span]
        row += s


def interleave(own, rest, cuts):
    shape = (2 * own.shape[0], own.shape[1])
    return pl.pallas_call(
        functools.partial(interleave_kernel, cuts),
        in_specs=[IN_VMEM] * 2,
        out_specs=IN_VMEM,
        out_shape=pltpu.VMEM(shape, BF),
        compiler_params=pltpu.CompilerParams(vmem_limit_bytes=VMEM_LIMIT),
        cost_estimate=pl.CostEstimate(flops=0, bytes_accessed=4 * shape[0] * shape[1], transcendentals=0),
        name="interleave",
    )(own, rest)


def place_kernel(tile_cols, flip, g_ref, _, out, buf, sems):
    row = lax.axis_index("row")
    width = buf.shape[0]
    col = tile_cols - 2 + (1 - row if flip else row)
    part = width // 2
    copies = []
    for k in range(2):
        span = slice(k * part, (k + 1) * part)
        buf[span] = g_ref[:, span].T
        to = pl.ds(pl.multiple_of(col * width + k * part, part), part)
        copies.append(pltpu.make_async_copy(buf.at[span], out.at[to], sems.at[k]))
        copies[-1].start()
    for copy in copies:
        copy.wait()


def place(out, column, tile_cols, flip):
    sources, width = column.shape
    return pl.pallas_call(
        functools.partial(place_kernel, tile_cols, flip),
        in_specs=[IN_VMEM, IN_HBM],
        out_specs=IN_HBM,
        out_shape=jax.ShapeDtypeStruct(out.shape, BF),
        scratch_shapes=[pltpu.VMEM((width, sources), BF), pltpu.SemaphoreType.DMA((2,))],
        input_output_aliases={1: 0},
        compiler_params=pltpu.CompilerParams(vmem_limit_bytes=VMEM_LIMIT),
        cost_estimate=pl.CostEstimate(flops=0, bytes_accessed=2 * sources * width, transcendentals=0),
        name="place",
    )(column, out)


def finish_kernel(plan, start, *refs):
    buf, sems = refs[-2:]
    out = refs[-3]
    width = buf.shape[1]
    copies = []
    for c, chunks in enumerate(plan):
        t = [refs[2 * k][at].astype(F32) + refs[2 * k + 1][at].astype(F32) for k, at in chunks]
        buf[c] = jnp.concatenate(t, axis=0).astype(BF).T
        copies.append(pltpu.make_async_copy(buf.at[c], out.at[pl.ds((start + c) * width, width)], sems.at[c]))
        copies[-1].start()
    for copy in copies:
        copy.wait()


def finish(out, chunks, start, count, rows, sources):
    flat, index, plan = [], {}, []
    for col in range(start, start + count):
        where = []
        for i, pieces in enumerate(chunks):
            for first, mine, got in pieces:
                if first <= col < first + mine.shape[0]:
                    if (i, first) not in index:
                        index[i, first] = len(flat) // 2
                        flat += [mine, got]
                    where.append((index[i, first], col - first))
        plan.append(where)
    width = flat[0].shape[2]
    specs = [IN_VMEM] * len(flat)
    aliases = {}
    if out is not None:
        aliases = {len(flat): 0}
        specs.append(IN_HBM)
        flat.append(out)
    return pl.pallas_call(
        functools.partial(finish_kernel, plan, start),
        in_specs=specs,
        out_specs=IN_HBM,
        out_shape=jax.ShapeDtypeStruct((rows, sources), BF),
        scratch_shapes=[pltpu.VMEM((count, width, sources), BF), pltpu.SemaphoreType.DMA((count,))],
        input_output_aliases=aliases,
        compiler_params=pltpu.CompilerParams(vmem_limit_bytes=VMEM_LIMIT),
        cost_estimate=pl.CostEstimate(flops=0, bytes_accessed=2 * count * sources * width, transcendentals=0),
        name="finish",
    )(*flat)


def solution(mesh):
    n_row, n_col = mesh.shape["row"], mesh.shape["col"]
    nz = n_col // 4
    assert n_col == 4 * nz and nz & (nz - 1) == 0
    core_swap = [(c, c ^ 1) for c in range(n_col)]
    x_swap = [(c, c ^ 2) for c in range(n_col)]
    z_swaps = [[(c, c ^ (4 * k)) for c in range(n_col)] for k in range(1, nz)]
    row_swap = [(0, 1), (1, 0)]

    def local(x_field, observed, sat_scale, u, v, ranks):
        tile_rows, tile_cols, _, _ = u.shape
        rows, sources = x_field.shape
        rb = observed.shape[0]
        zs = nz // tile_rows
        cuts = tuple(c * sources // 256 for c in CUTS)
        sat = sat_scale[:, None]
        odd = lax.rem(lax.div(lax.axis_index("col"), 4), 2) == 1
        shared = n_row == 2
        keeps, sends, early = forward(x_field, observed, u, v, ranks, cuts, zs, shared)
        cols = tile_cols - 2 if shared else tile_cols
        if shared:
            theirs = lax.ppermute(early[0], "row", row_swap)
        u = hold(u, 0)
        v = hold(v, 2 * u.size)

        def residual(send, keep, sc):
            got = lax.ppermute(send, "col", core_swap)
            half = keep + got.astype(F32)
            got = lax.ppermute(half[1].astype(BF), "col", x_swap)
            quarter = half[0] + got.astype(F32)
            mine = quarter.astype(BF)
            total = quarter
            for p in z_swaps:
                total = total + lax.ppermute(mine, "col", p).astype(F32)
            r00 = (sc * jnp.tanh(total / sc)).astype(BF)
            r01 = lax.ppermute(r00, "col", x_swap)
            if shared:
                part = jnp.where(odd, r00[r00.shape[0] // 2 :], r00[: r00.shape[0] // 2]) if nz > 1 else r00
                other.append(lax.ppermute(part, "row", row_swap))
            return (r00, r01) + gather(r00, r01)

        def gather(r00, r01):
            return lax.ppermute(r00, "col", core_swap), lax.ppermute(r01, "col", core_swap)

        swapped = [[] for _ in cuts]
        resids, other = [], []
        row = 0
        for i, s in enumerate(cuts):
            resid = residual(sends[i], keeps[i], sat[row : row + s])
            resids.append(resid)
            row += s
            start = 0
            for g in range(len(GROUPS[i])):
                per = sum(GROUPS[i][: g + 1]) * cols // sum(GROUPS[i]) - start
                part = adjoint(resid, u, v, ranks, start, per, rb, zs)
                if n_row == 2:
                    swapped[i].append((start, part, lax.ppermute(part, "row", row_swap)))
                else:
                    whole = lax.psum(part.astype(F32), "row").astype(BF)
                    swapped[i].append((start, whole, jnp.zeros_like(whole)))
                start += per
        if shared:
            r00 = join(other)
            if nz > 1:
                rest = lax.ppermute(r00, "col", z_swaps[0])
                r00 = interleave(r00, rest, cuts)
            r01 = lax.ppermute(r00, "col", x_swap)
            blocks = (r00, r01) + gather(r00, r01)
            column = pair_column(resids, blocks, theirs, u, v, ranks, rb, zs)
            column_got = lax.ppermute(column, "row", row_swap)
        out = None
        for start, part, _ in swapped[-1]:
            out = finish(out, swapped, start, part.shape[0], rows, sources)
        if shared:
            out = place(out, column, tile_cols, False)
            out = place(out, column_got, tile_cols, True)
        return out

    return jax.shard_map(
        local,
        mesh=mesh,
        in_specs=(
            P("col", None),
            P(("row", "col"), None),
            P(),
            P("row", "col", None, None),
            P("row", "col", None, None),
            P("row", "col"),
        ),
        out_specs=P("col", None),
        check_vma=False,
    )
```

```python
import functools
import math

import jax
import jax.numpy as jnp
from jax import lax
from jax.experimental import pallas as pl
from jax.experimental.pallas import tpu as pltpu
from jax.sharding import PartitionSpec as P


BF = jnp.bfloat16
F32 = jnp.float32
CUTS = (128, 128)
GROUPS = ((3, 3), (3, 3))
VMEM_LIMIT = 26 * 2**20
IN_VMEM = pl.BlockSpec(memory_space=pltpu.VMEM)
IN_SMEM = pl.BlockSpec(memory_space=pltpu.SMEM)
IN_HBM = pl.BlockSpec(memory_space=pltpu.HBM)


def dot_nn(a, b):
    return lax.dot_general(a, b, (((1,), (0,)), ((), ())), preferred_element_type=F32)


def dot_nt(a, b):
    return lax.dot_general(a, b, (((1,), (1,)), ((), ())), preferred_element_type=F32)


def permuted_rows(tile, zs, rb):
    return jnp.concatenate(
        [tile[(z * 4 + q) * rb : (z * 4 + q + 1) * rb] for q in range(4) for z in range(zs)], axis=0
    )


def position():
    col = lax.axis_index("col")
    return lax.rem(col, 2), lax.rem(lax.div(col, 2), 2), lax.div(col, 4)


def forward_kernel(dims, ranks, obs, x_hbm, u_hbm, v_hbm, *rest):
    tile_rows, tile_cols, width, cap, sources, rb, zs, cuts, shared = dims
    n = len(cuts)
    keep_refs, send_refs = rest[:n], rest[n : 2 * n]
    x_vm, u_vm, v_vm, acc, sems = rest[-5:]

    def copies(j, first):
        span = pl.ds(j * width, width)
        if first:
            pairs = [(x_hbm.at[span], x_vm.at[span])] + [(v_hbm.at[a, j], v_vm.at[a, j]) for a in range(tile_rows)]
        else:
            pairs = [(u_hbm.at[a, j], u_vm.at[a, j]) for a in range(tile_rows)]
        base = 0 if first else 1 + tile_rows
        return [pltpu.make_async_copy(src, dst, sems.at[j, base + k]) for k, (src, dst) in enumerate(pairs)]

    jb = 2 if tile_cols % 2 == 0 else 1
    steps = [tuple(range(j, j + jb)) for j in range(0, tile_cols, jb)][::-1]
    if jb == 2:
        steps[-1:] = [(1,), (0,)]
    for step in steps:
        for j in step:
            for c in copies(j, True) + copies(j, False):
                c.start()

    mine, my_x, my_z = position()
    lane = lax.broadcasted_iota(jnp.int32, (sources, cap), 1)
    early_copies = []
    last = []
    for step in steps:
        parts = [[] for _ in range(tile_rows)]
        for j in step:
            for c in copies(j, True) + copies(j, False):
                c.wait()
            xt = x_vm[j * width : (j + 1) * width, :].T
            for a in range(tile_rows):
                c = dot_nn(xt, v_vm[a, j])
                parts[a].append(jnp.where(lane < ranks[a, j], c, 0.0).astype(BF))
        for a in range(tile_rows):
            w = jnp.concatenate([permuted_rows(u_vm[a, j], zs, rb) for j in step], axis=1)
            p = dot_nt(jnp.concatenate(parts[a], axis=1), w)
            if step == steps[0]:
                acc[a] = p
            elif step == steps[-1]:
                last.append(p)
            else:
                acc[a] += p
        if shared and step == steps[0]:
            early, masked, early_sems = rest[2 * n : 2 * n + 3]
            col = tile_cols - 1 - lax.axis_index("row")
            rank_lane = lax.broadcasted_iota(jnp.int32, (width, cap), 1)
            for a in range(tile_rows):
                masked[a] = jnp.where(rank_lane < ranks[a, col], u_vm[a, col], jnp.zeros((), BF))
                early_copies.append(pltpu.make_async_copy(masked.at[a], early.at[0, a], early_sems.at[0, a]))
                early_copies.append(pltpu.make_async_copy(v_vm.at[a, col], early.at[1, a], early_sems.at[1, a]))
            for c in early_copies:
                c.start()

    nz = zs * tile_rows
    q_lanes = width // 4
    obs_t = obs[...].astype(F32).T
    obs_t = jnp.concatenate([obs_t] * nz, axis=1)
    spot = lax.broadcasted_iota(jnp.int32, (sources, nz * rb), 1)
    obs_t = jnp.where((spot >= my_z * rb) & (spot < (my_z + 1) * rb), obs_t, 0.0)
    for q in range(4):
        qx, qc = q // 2, q % 2
        slot = qx ^ my_x
        row = 0
        for i, s in enumerate(cuts):
            val = jnp.concatenate(
                [
                    acc[a, row : row + s, q * q_lanes : (q + 1) * q_lanes]
                    + last[a][row : row + s, q * q_lanes : (q + 1) * q_lanes]
                    for a in range(tile_rows)
                ],
                axis=1,
            )

            @pl.when(mine == qc)
            def _():
                own = jnp.where(slot == 0, 1.0, 0.0).astype(F32)
                keep_refs[i][slot] = val - own * obs_t[row : row + s]

            @pl.when(mine != qc)
            def _():
                send_refs[i][slot] = val.astype(BF)

            row += s
    for c in early_copies:
        c.wait()


def forward(x, obs, u, v, ranks, cuts, zs, shared):
    tile_rows, tile_cols, width, cap = u.shape
    sources = x.shape[1]
    rb = obs.shape[0]
    block = tile_rows * width // 4
    dims = (tile_rows, tile_cols, width, cap, sources, rb, zs, cuts, shared)
    outs = [pltpu.VMEM((2, s, block), F32) for s in cuts] + [pltpu.VMEM((2, s, block), BF) for s in cuts]
    out_specs = [IN_VMEM] * len(outs)
    extra = []
    if shared:
        outs.append(pltpu.VMEM((2, tile_rows, width, cap), BF))
        out_specs.append(pl.BlockSpec(memory_space=pl.ANY))
        extra = [pltpu.VMEM((tile_rows, width, cap), BF), pltpu.SemaphoreType.DMA((2, tile_rows))]
    room = 2**20 + sum(math.prod(o.shape) * o.dtype.itemsize for o in outs)
    res = pl.pallas_call(
        functools.partial(forward_kernel, dims),
        in_specs=[IN_SMEM, IN_VMEM, IN_HBM, IN_HBM, IN_HBM],
        out_specs=out_specs,
        scratch_shapes=extra
        + [
            pltpu.VMEM(x.shape, BF),
            pltpu.VMEM(u.shape, BF),
            pltpu.VMEM(v.shape, BF),
            pltpu.VMEM((tile_rows, sources, width), F32),
            pltpu.SemaphoreType.DMA((tile_cols, 1 + 2 * tile_rows)),
        ],
        out_shape=outs,
        compiler_params=pltpu.CompilerParams(vmem_limit_bytes=63 * 2**20 - room),
        cost_estimate=pl.CostEstimate(
            flops=4 * tile_rows * tile_cols * width * cap * sources,
            bytes_accessed=4 * u.size + 2 * x.size,
            transcendentals=0,
        ),
        name="forward",
    )(ranks, obs, x, u, v)
    n = len(cuts)
    return res[:n], res[n : 2 * n], res[2 * n :]


def hold_kernel(src, dst, sem):
    copy = pltpu.make_async_copy(src, dst, sem)
    copy.start()
    copy.wait()


def hold(array, before):
    room = before + 2 * array.size + 3 * 2**20
    return pl.pallas_call(
        hold_kernel,
        in_specs=[IN_HBM],
        out_specs=pl.BlockSpec(memory_space=pl.ANY),
        out_shape=pltpu.VMEM(array.shape, array.dtype),
        scratch_shapes=[pltpu.SemaphoreType.DMA],
        compiler_params=pltpu.CompilerParams(vmem_limit_bytes=63 * 2**20 - room),
        cost_estimate=pl.CostEstimate(flops=0, bytes_accessed=2 * array.size, transcendentals=0),
        name="hold",
    )(array)


def adjoint_kernel(dims, ranks, r00, r01, r10, r11, u_ref, v_ref, g_ref, held):
    tile_rows, _, start, count, width, cap, s, rb, zs = dims
    mine, my_x, _ = position()
    base = my_x * 2 + mine
    held[base] = r00[...]
    held[base ^ 2] = r01[...]
    held[base ^ 1] = r10[...]
    held[base ^ 3] = r11[...]
    q_lanes = width // 4
    lane = lax.broadcasted_iota(jnp.int32, (s, cap), 1)
    r = [
        jnp.concatenate([held[q][:, a * q_lanes : (a + 1) * q_lanes] for q in range(4)], axis=1)
        for a in range(tile_rows)
    ]
    for j in range(count):
        total = None
        for a in range(tile_rows):
            adj = dot_nn(r[a], permuted_rows(u_ref[a, start + j], zs, rb))
            adj = jnp.where(lane < ranks[a, start + j], adj, 0.0).astype(BF)
            g = dot_nt(adj, v_ref[a, start + j])
            total = g if total is None else total + g
        g_ref[j] = total.astype(BF)


def adjoint(rs, u, v, ranks, start, count, rb, zs):
    tile_rows, tile_cols, width, cap = u.shape
    s, block = rs[0].shape
    dims = (tile_rows, tile_cols, start, count, width, cap, s, rb, zs)
    return pl.pallas_call(
        functools.partial(adjoint_kernel, dims),
        in_specs=[IN_SMEM] + [IN_VMEM] * 6,
        out_specs=IN_VMEM,
        scratch_shapes=[pltpu.VMEM((4, s, block), BF)],
        out_shape=jax.ShapeDtypeStruct((count, s, width), BF),
        compiler_params=pltpu.CompilerParams(vmem_limit_bytes=VMEM_LIMIT),
        cost_estimate=pl.CostEstimate(
            flops=4 * tile_rows * count * width * cap * s, bytes_accessed=4 * s * block, transcendentals=0
        ),
        name="adjoint",
    )(ranks, *rs, u, v)


def pair_kernel(dims, ranks, *refs):
    tile_rows, tile_cols, width, cap, cuts, rb, zs = dims
    n = len(cuts)
    other = refs[4 * n : 4 * n + 4]
    got, u_ref, v_ref, g_ref, held, theirs = refs[4 * n + 4 :]
    mine, my_x, _ = position()
    base = my_x * 2 + mine
    for k, bits in enumerate((0, 2, 1, 3)):
        row = 0
        for i, s in enumerate(cuts):
            held[base ^ bits, row : row + s] = refs[4 * i + k][...]
            row += s
        theirs[base ^ bits] = other[k][...]
    col = tile_cols - 2 + lax.axis_index("row")
    q_lanes = width // 4
    sources = held.shape[1]
    lane = lax.broadcasted_iota(jnp.int32, (sources, cap), 1)
    total = None
    for a in range(tile_rows):
        span = slice(a * q_lanes, (a + 1) * q_lanes)
        r = jnp.concatenate([held[q][:, span] for q in range(4)], axis=1)
        adj = dot_nn(r, permuted_rows(u_ref[a, col], zs, rb))
        adj = jnp.where(lane < ranks[a, col], adj, 0.0).astype(BF)
        g = dot_nt(adj, v_ref[a, col])
        total = g if total is None else total + g
        r = jnp.concatenate([theirs[q][:, span] for q in range(4)], axis=1)
        adj = dot_nn(r, permuted_rows(got[0, a], zs, rb)).astype(BF)
        total = total + dot_nt(adj, got[1, a])
    g_ref[...] = total.T.astype(BF)


def pair_column(resid, other, got, u, v, ranks, rb, zs):
    tile_rows, tile_cols, width, cap = u.shape
    cuts = tuple(rs[0].shape[0] for rs in resid)
    sources, block = other[0].shape
    dims = (tile_rows, tile_cols, width, cap, cuts, rb, zs)
    flat = [r for rs in resid for r in rs] + list(other)
    return pl.pallas_call(
        functools.partial(pair_kernel, dims),
        in_specs=[IN_SMEM] + [IN_VMEM] * (len(flat) + 3),
        out_specs=IN_VMEM,
        scratch_shapes=[pltpu.VMEM((4, sources, block), BF)] * 2,
        out_shape=pltpu.VMEM((width, sources), BF),
        compiler_params=pltpu.CompilerParams(vmem_limit_bytes=VMEM_LIMIT),
        cost_estimate=pl.CostEstimate(
            flops=8 * tile_rows * width * cap * sources, bytes_accessed=4 * sources * block, transcendentals=0
        ),
        name="pair",
    )(ranks, *flat, got, u, v)


def join_kernel(*refs):
    row = 0
    for r in refs[:-1]:
        refs[-1][row : row + r.shape[0]] = r[...]
        row += r.shape[0]


def join(parts):
    shape = (sum(p.shape[0] for p in parts), parts[0].shape[1])
    return pl.pallas_call(
        join_kernel,
        in_specs=[IN_VMEM] * len(parts),
        out_specs=IN_VMEM,
        out_shape=pltpu.VMEM(shape, BF),
        compiler_params=pltpu.CompilerParams(vmem_limit_bytes=VMEM_LIMIT),
        cost_estimate=pl.CostEstimate(flops=0, bytes_accessed=4 * shape[0] * shape[1], transcendentals=0),
        name="join",
    )(*parts)


def interleave_kernel(cuts, own, rest, out):
    odd = lax.rem(lax.div(lax.axis_index("col"), 4), 2)
    row = 0
    for s in cuts:
        half = s // 2
        span = slice(row // 2, row // 2 + half)
        out[pl.ds(pl.multiple_of(row + odd * half, 16), half)] = own[span]
        out[pl.ds(pl.multiple_of(row + (1 - odd) * half, 16), half)] = rest[span]
        row += s


def interleave(own, rest, cuts):
    shape = (2 * own.shape[0], own.shape[1])
    return pl.pallas_call(
        functools.partial(interleave_kernel, cuts),
        in_specs=[IN_VMEM] * 2,
        out_specs=IN_VMEM,
        out_shape=pltpu.VMEM(shape, BF),
        compiler_params=pltpu.CompilerParams(vmem_limit_bytes=VMEM_LIMIT),
        cost_estimate=pl.CostEstimate(flops=0, bytes_accessed=4 * shape[0] * shape[1], transcendentals=0),
        name="interleave",
    )(own, rest)


def place_kernel(tile_cols, flip, g_ref, _, out, sem):
    row = lax.axis_index("row")
    width = g_ref.shape[0]
    col = tile_cols - 2 + (1 - row if flip else row)
    copy = pltpu.make_async_copy(g_ref, out.at[pl.ds(pl.multiple_of(col * width, width), width)], sem)
    copy.start()
    copy.wait()


def place(out, column, tile_cols, flip):
    width, sources = column.shape
    return pl.pallas_call(
        functools.partial(place_kernel, tile_cols, flip),
        in_specs=[IN_VMEM, IN_HBM],
        out_specs=IN_HBM,
        out_shape=jax.ShapeDtypeStruct(out.shape, BF),
        scratch_shapes=[pltpu.SemaphoreType.DMA],
        input_output_aliases={1: 0},
        compiler_params=pltpu.CompilerParams(vmem_limit_bytes=VMEM_LIMIT),
        cost_estimate=pl.CostEstimate(flops=0, bytes_accessed=2 * sources * width, transcendentals=0),
        name="place",
    )(column, out)


def finish_kernel(plan, start, *refs):
    buf, sems = refs[-2:]
    out = refs[-3]
    width = buf.shape[1]
    copies = []
    for c, chunks in enumerate(plan):
        t = [refs[2 * k][at].astype(F32) + refs[2 * k + 1][at].astype(F32) for k, at in chunks]
        buf[c] = jnp.concatenate(t, axis=0).astype(BF).T
        copies.append(pltpu.make_async_copy(buf.at[c], out.at[pl.ds((start + c) * width, width)], sems.at[c]))
        copies[-1].start()
    for copy in copies:
        copy.wait()


def finish(out, chunks, start, count, rows, sources):
    flat, index, plan = [], {}, []
    for col in range(start, start + count):
        where = []
        for i, pieces in enumerate(chunks):
            for first, mine, got in pieces:
                if first <= col < first + mine.shape[0]:
                    if (i, first) not in index:
                        index[i, first] = len(flat) // 2
                        flat += [mine, got]
                    where.append((index[i, first], col - first))
        plan.append(where)
    width = flat[0].shape[2]
    specs = [IN_VMEM] * len(flat)
    aliases = {}
    if out is not None:
        aliases = {len(flat): 0}
        specs.append(IN_HBM)
        flat.append(out)
    return pl.pallas_call(
        functools.partial(finish_kernel, plan, start),
        in_specs=specs,
        out_specs=IN_HBM,
        out_shape=jax.ShapeDtypeStruct((rows, sources), BF),
        scratch_shapes=[pltpu.VMEM((count, width, sources), BF), pltpu.SemaphoreType.DMA((count,))],
        input_output_aliases=aliases,
        compiler_params=pltpu.CompilerParams(vmem_limit_bytes=VMEM_LIMIT),
        cost_estimate=pl.CostEstimate(flops=0, bytes_accessed=2 * count * sources * width, transcendentals=0),
        name="finish",
    )(*flat)


def solution(mesh):
    n_row, n_col = mesh.shape["row"], mesh.shape["col"]
    nz = n_col // 4
    assert n_col == 4 * nz and nz & (nz - 1) == 0
    core_swap = [(c, c ^ 1) for c in range(n_col)]
    x_swap = [(c, c ^ 2) for c in range(n_col)]
    z_swaps = [[(c, c ^ (4 * k)) for c in range(n_col)] for k in range(1, nz)]
    row_swap = [(0, 1), (1, 0)]

    def local(x_field, observed, sat_scale, u, v, ranks):
        tile_rows, tile_cols, _, _ = u.shape
        rows, sources = x_field.shape
        rb = observed.shape[0]
        zs = nz // tile_rows
        cuts = tuple(c * sources // 256 for c in CUTS)
        sat = sat_scale[:, None]
        odd = lax.rem(lax.div(lax.axis_index("col"), 4), 2) == 1
        shared = n_row == 2
        keeps, sends, early = forward(x_field, observed, u, v, ranks, cuts, zs, shared)
        cols = tile_cols - 2 if shared else tile_cols
        if shared:
            theirs = lax.ppermute(early[0], "row", row_swap)
        u = hold(u, 0)
        v = hold(v, 2 * u.size)

        def residual(send, keep, sc):
            got = lax.ppermute(send, "col", core_swap)
            half = keep + got.astype(F32)
            got = lax.ppermute(half[1].astype(BF), "col", x_swap)
            quarter = half[0] + got.astype(F32)
            mine = quarter.astype(BF)
            total = quarter
            for p in z_swaps:
                total = total + lax.ppermute(mine, "col", p).astype(F32)
            r00 = (sc * jnp.tanh(total / sc)).astype(BF)
            r01 = lax.ppermute(r00, "col", x_swap)
            if shared:
                part = jnp.where(odd, r00[r00.shape[0] // 2 :], r00[: r00.shape[0] // 2]) if nz > 1 else r00
                other.append(lax.ppermute(part, "row", row_swap))
            return (r00, r01) + gather(r00, r01)

        def gather(r00, r01):
            return lax.ppermute(r00, "col", core_swap), lax.ppermute(r01, "col", core_swap)

        swapped = [[] for _ in cuts]
        resids, other = [], []
        row = 0
        for i, s in enumerate(cuts):
            resid = residual(sends[i], keeps[i], sat[row : row + s])
            resids.append(resid)
            row += s
            start = 0
            for g in range(len(GROUPS[i])):
                per = sum(GROUPS[i][: g + 1]) * cols // sum(GROUPS[i]) - start
                part = adjoint(resid, u, v, ranks, start, per, rb, zs)
                if n_row == 2:
                    swapped[i].append((start, part, lax.ppermute(part, "row", row_swap)))
                else:
                    whole = lax.psum(part.astype(F32), "row").astype(BF)
                    swapped[i].append((start, whole, jnp.zeros_like(whole)))
                start += per
        if shared:
            r00 = join(other)
            if nz > 1:
                rest = lax.ppermute(r00, "col", z_swaps[0])
                r00 = interleave(r00, rest, cuts)
            r01 = lax.ppermute(r00, "col", x_swap)
            blocks = (r00, r01) + gather(r00, r01)
            column = pair_column(resids, blocks, theirs, u, v, ranks, rb, zs)
            column_got = lax.ppermute(column, "row", row_swap)
        out = None
        for start, part, _ in swapped[-1]:
            out = finish(out, swapped, start, part.shape[0], rows, sources)
        if shared:
            out = place(out, column, tile_cols, False)
            out = place(out, column_got, tile_cols, True)
        return out

    return jax.shard_map(
        local,
        mesh=mesh,
        in_specs=(
            P("col", None),
            P(("row", "col"), None),
            P(),
            P("row", "col", None, None),
            P("row", "col", None, None),
            P("row", "col"),
        ),
        out_specs=P("col", None),
        check_vma=False,
    )
```
